32 devices in a mesh: dp: 8 (over y, x, core), ctx: 4 (over z).
Axes of the slice: x: 2, y: 2, z: 4, core: 2. Of those that a mesh axis runs over, the one named last changes fastest.
Arguments:
- queries: bfloat16 [6144, 2048], P(('dp', 'ctx')), parts along dimension 0, may hold values from -6 to 6
- keys: bfloat16 [6144, 2048], P(('dp', 'ctx')), parts along dimension 0, may hold values from -6 to 6
- values: bfloat16 [6144, 2048], P(('dp', 'ctx')), parts along dimension 0, may hold values from -6 to 6
- beta: float32 [6144, 16], P(('dp', 'ctx')), parts along dimension 0, may hold values from 0.01 to 0.1
- log_decay: bfloat16 [6144, 2048], P(('dp', 'ctx')), parts along dimension 0, may hold values from -0.6 to 0
- out_gain: float32 [2048], replicated, may hold values from 0.25 to 1.75
- doc_lengths: int32 [128], P('dp'), parts along dimension 0, may hold values from 1 to 384, 768 in all
Outputs:
- mixed: bfloat16 [6144, 2048], P(('dp', 'ctx')), parts along dimension 0
The draws below stay inside these ranges and needn't reach their ends.
There are 8 independent parts, one for each index of `dp`. The reference program is written for one: setup_inputs(seed, part) draws one part's arguments, and reference() takes and returns one part's arrays. A program takes and returns all parts, laid end to end along the dimension named above; an argument that names none is the same for every part. Nothing has to cross between parts.
All inputs are finite; a program needn't handle non-finite values.
Results may differ from the reference program's by a relative error of at most 0.001.
Values sent between devices are 32-bit elements; how exact they have to be, the bound alone decides.
No kernel may reach another device: no remote copies, remote signals or barrier semaphores. Data moves between devices by JAX's collectives and lax.ppermute only.
A program may use at most 128 MiB of HBM per device.

```python
import math
import jax
import jax.numpy as jnp
import numpy as np
from jax import lax

H = 16
DK = 128
DV = 128
NDOCS = 16
STREAM_TOKENS = 768
DOC_MOST = 384


def draw_log_decay(key, part):
    key_sequence = jax.random.split(key, 7)
    fast_share = 0.5
    fast_heads = jax.random.uniform(key_sequence[0], (H,)) < fast_share
    slow_rate = jnp.exp(jax.random.uniform(key_sequence[1], (H, DK), minval=math.log(0.1), maxval=math.log(0.6))) / STREAM_TOKENS
    fast_rate = jnp.exp(jax.random.uniform(key_sequence[2], (H, DK), minval=math.log(1.0 / 50.0), maxval=math.log(1.0 / 20.0)))
    decay_rates = jnp.where(fast_heads[:, None], fast_rate, slow_rate)
    approximate_output = jax.random.uniform(key_sequence[3], (STREAM_TOKENS, H, DK), minval=0.5, maxval=2.0)
    half_stream = STREAM_TOKENS // 2
    first_place = jax.random.randint(key_sequence[4], (1,), 0, half_stream)
    second_place = jax.random.randint(key_sequence[6], (1,), half_stream, STREAM_TOKENS)
    group_position = jnp.concatenate([first_place, second_place])
    group_depth = jax.random.uniform(key_sequence[5], (2,), minval=0.22, maxval=0.49)
    matched_rows = (jnp.arange(STREAM_TOKENS)[:, None] == group_position[None, :]).astype(jnp.float32)
    document_group = jnp.sum(matched_rows * group_depth[None, :], axis=1)
    value_current = -(decay_rates[None] * approximate_output) - document_group[:, None, None]
    return value_current.reshape(STREAM_TOKENS, H * DK).astype(jnp.bfloat16)


def block_levels(key, shape, pieces, least, largest):
    gain, own = 1.0, jax.random.fold_in(key, 6)
    for position, shards_of in pieces:
        draws = jnp.exp(jax.random.uniform(jax.random.fold_in(own, position), (shards_of,), jnp.float32, least / len(pieces), largest / len(pieces)))
        gain = gain * jnp.repeat(draws, shape[position] // shards_of).reshape([-1 if axis == position else 1 for axis in range(len(shape))])
    return gain


def length_profile(count, total, limit, lean):
    portions = [(1 << 20) // math.isqrt(grade ** lean) + 1 for grade in range(2, count + 1)]
    spare, given = total - limit - (count - 1), [1] * (count - 1)
    while spare > 0:
        candidates = [i for i in range(count - 1) if given[i] < limit]
        mass, left = sum([portions[i] for i in candidates]), spare
        for i in candidates:
            more = min(limit - given[i], max(1, left * portions[i] // mass), spare)
            given[i] = given[i] + more
            spare = spare - more
    return np.array([limit] + given)


def uneven(stream_key, number_of, total, reach, slope):
    if number_of == 2:
        one = jax.random.randint(stream_key, (), max(1, total - reach), min(reach, total - 1) + 1)
        return jnp.stack([one, total - one])
    lengths = jnp.asarray(length_profile(number_of, total, reach, slope), jnp.int32)
    twos = (number_of - 1) // 2
    source_of, taker = lengths[1:1 + 2 * twos:2], lengths[2:2 + 2 * twos:2]
    slack = jnp.minimum(source_of - 1, reach - taker)
    shifted = jax.random.randint(jax.random.fold_in(stream_key, 1), (twos,), 0, 1 << 20) % (slack + 1)
    lengths = lengths.at[1:1 + 2 * twos:2].set(source_of - shifted).at[2:2 + 2 * twos:2].set(taker + shifted)
    return lengths[jax.random.permutation(jax.random.fold_in(stream_key, 2), number_of)]


def centred(rng, shape, width, reach, pieces=(), kind=jnp.bfloat16):
    values = width * jax.random.normal(rng, shape, jnp.float32)
    if pieces:
        values = values * block_levels(rng, shape, pieces, -0.22, 0.18)
    return jnp.clip(values, -reach, reach).astype(kind)


def setup_inputs(seed: int = 0, part: int = 0) -> dict:
    splits = jax.random.split(jax.random.key(seed), 8)
    own_keys = jax.random.split(jax.random.fold_in(splits[7], part), 8)
    queries = centred(own_keys[0], (STREAM_TOKENS, H * DK), 1.0, 6.0, ((0, 4),))
    keys = centred(own_keys[1], (STREAM_TOKENS, H * DK), 1.0, 6.0, ((0, 4),))
    values = centred(own_keys[2], (STREAM_TOKENS, H * DV), 1.0, 6.0, ((0, 4),))
    beta = jnp.clip(jnp.exp(math.log(0.1) - 2.3025851 * jax.random.uniform(own_keys[3], (STREAM_TOKENS, H), jnp.float32) ** block_levels(own_keys[3], (STREAM_TOKENS, H), ((0, 4),), -0.2, 0.2)), 0.01, 0.1)
    log_decay = draw_log_decay(jax.random.fold_in(jax.random.fold_in(splits[7], part), 71), part)
    out_gain = jnp.clip(1.0 + 0.15 * jax.random.normal(splits[5], (H * DV,), jnp.float32), 0.25, 1.75)
    doc_lengths = uneven(own_keys[6], NDOCS, STREAM_TOKENS, DOC_MOST, 2).astype(jnp.int32)
    return {"queries": queries, "keys": keys, "values": values, "beta": beta, "log_decay": log_decay, "out_gain": out_gain, "doc_lengths": doc_lengths}


HIGHEST_ACCURACY = lax.Precision.HIGHEST

def unit_rows(x):
    return x / jnp.sqrt(lax.optimization_barrier(jnp.sum(x * x, axis=-1, keepdims=True)) + 1e-06)

def reference(queries, keys, values, beta, log_decay, out_gain, doc_lengths):
    qn = unit_rows(queries.astype(jnp.float32).reshape(STREAM_TOKENS, H, DK))
    kn = unit_rows(keys.astype(jnp.float32).reshape(STREAM_TOKENS, H, DK))
    vals = values.astype(jnp.float32).reshape(STREAM_TOKENS, H, DV)
    alpha = jnp.exp(log_decay.astype(jnp.float32).reshape(STREAM_TOKENS, H, DK))
    starts = (jnp.cumsum(doc_lengths) - doc_lengths).astype(jnp.int32)
    place = jnp.arange(STREAM_TOKENS, dtype=jnp.int32)
    resets = lax.optimization_barrier(jnp.sum((place[:, None] == starts[None, :]).astype(jnp.float32), axis=1))
    keeping = 1.0 - jnp.minimum(resets, 1.0)

    def advance(memory_state, item):
        query_current, key_current, v_t, b_t, a_t, keep_t = item
        decayed_state = memory_state * (a_t * keep_t)[:, :, None]
        estimated_output = jnp.einsum('yq,yqc->yc', key_current, decayed_state, precision=HIGHEST_ACCURACY)
        update = b_t[:, None] * (v_t - estimated_output)
        memory_state = decayed_state + key_current[:, :, None] * update[:, None, :]
        output_rows = jnp.einsum('yq,yqc->yc', query_current, memory_state, precision=HIGHEST_ACCURACY)
        return (memory_state, output_rows)
    state0 = jnp.zeros((H, DK, DV), jnp.float32)
    _, outs = lax.scan(advance, state0, (qn, kn, vals, beta.astype(jnp.float32), alpha, keeping))
    scale = jnp.sqrt(lax.optimization_barrier(jnp.mean(outs * outs, axis=-1, keepdims=True)) + 1e-06)
    normed = outs / scale * out_gain.astype(jnp.float32).reshape(H, DV)[None]
    return normed.reshape(STREAM_TOKENS, H * DV).astype(jnp.bfloat16)
```

```python
import functools

import jax
import jax.numpy as jnp
from jax import lax
from jax.experimental import pallas as pl
from jax.experimental.pallas import tpu as pltpu
from jax.sharding import PartitionSpec as P

F32 = jnp.float32
BF16 = jnp.bfloat16
TILE = 32
BLOCK = 64
TOGETHER = 2


def halves(x):
    high = x.astype(BF16)
    return high, (x - high.astype(F32)).astype(BF16)


def dot(a, b, dims=((1,), (0,))):
    return lax.dot_general(a, b, (dims, ((), ())), preferred_element_type=F32)


def dot3(a, b, dims=((1,), (0,))):
    return dot(a[0], b[0], dims) + (dot(a[0], b[1], dims) + dot(a[1], b[0], dims))


def rows_of(pair, low, high):
    return pair[0][low:high], pair[1][low:high]


def unit_rows(x):
    return x * lax.rsqrt(jnp.sum(x * x, axis=-1, keepdims=True) + 1e-06)


def doc_ids(lengths_ref, first, shape, dim):
    docs = lengths_ref.shape[0]
    place = first + lax.broadcasted_iota(jnp.int32, shape, dim)
    ids = jnp.zeros(shape, jnp.int32)
    before = jnp.int32(0)
    start = jnp.int32(0)
    for d in range(docs):
        ids = ids + (place >= start).astype(jnp.int32)
        before = before + (first > start).astype(jnp.int32)
        start = start + lengths_ref[d]
    return ids, before


def tile_inverse(system, count):
    lane = lax.broadcasted_iota(jnp.int32, (TILE, count), 1)
    row = lax.broadcasted_iota(jnp.int32, (TILE, count), 0)
    side = jnp.zeros((TILE, count), F32)
    for b in range(count // TILE):
        side = jnp.where(lane // TILE == b, system[b * TILE : (b + 1) * TILE, :], side)
    parts = []
    for low in range(0, count, 128):
        high = min(low + 128, count)
        piece = side[:, low:high]
        if high - low < 128:
            piece = jnp.concatenate([piece, jnp.zeros((TILE, 128 - high + low), F32)], axis=1)
        lanes = lax.broadcasted_iota(jnp.int32, (TILE, 128), 1)
        home = lanes - lanes % TILE
        inverse = (lanes % TILE == lax.broadcasted_iota(jnp.int32, (TILE, 128), 0)).astype(F32)
        for j in range(TILE - 1):
            top = (j + 1) // 8 * 8
            column = jnp.take_along_axis(piece[top:], (home + j)[top:], axis=1, mode="promise_in_bounds")
            lower = inverse[top:] - column * inverse[j : j + 1, :]
            inverse = lower if top == 0 else jnp.concatenate([inverse[:top], lower], axis=0)
        parts.append(inverse[:, : high - low])
    return jnp.concatenate(parts, axis=1)


def spread(side, count, height, column_of):
    lane = lax.broadcasted_iota(jnp.int32, side.shape, 1)
    return jnp.concatenate(
        [jnp.where(column_of(lane) == b, side, 0.0) for b in range(count // height)], axis=0
    )


def block_inverses(system, count):
    small = tile_inverse(system, count)
    lane = lax.broadcasted_iota(jnp.int32, small.shape, 1)
    even = lane // TILE % 2 == 0
    below = jnp.zeros(small.shape, F32)
    for b in range(1, count // TILE, 2):
        below = jnp.where(lane // TILE == b - 1, system[b * TILE : (b + 1) * TILE, :], below)
    wide = spread(small, count, TILE, lambda x: x // TILE)
    middle = dot3(halves(below), halves(wide))
    tall = spread(middle, count, TILE, lambda x: jnp.where(x // TILE % 2 == 0, x // TILE + 1, -1))
    odd = jnp.where(even, 0.0, small)
    corner = dot3(halves(odd), halves(tall))
    return jnp.concatenate([jnp.where(even, small, 0.0), jnp.where(even, -corner, small)], axis=0)


def solve(system, right, count):
    inverses = block_inverses(system, count)
    split_system = halves(system)
    done = None
    for b in range(count // BLOCK):
        low, high = b * BLOCK, (b + 1) * BLOCK
        part = right[low:high]
        if b:
            left = tuple(x[low:high, :low] for x in split_system)
            part = part - dot3(left, done)
        result = halves(dot3(halves(inverses[:, low:high]), halves(part)))
        done = result if b == 0 else tuple(jnp.concatenate(x, axis=0) for x in zip(done, result))
    return done


def span_kernel(lengths_ref, q_ref, k_ref, v_ref, beta_ref, g_ref, a_ref, b_ref, out_ref, reach_ref):
    count = q_ref.shape[0]
    width = q_ref.shape[1] // TOGETHER
    first = lax.axis_index("ctx") * count
    ids_col, before = doc_ids(lengths_ref, first, (count, 1), 0)
    ids_row, _ = doc_ids(lengths_ref, first, (1, count), 1)
    row = lax.broadcasted_iota(jnp.int32, (count, count), 0)
    col = lax.broadcasted_iota(jnp.int32, (count, count), 1)
    same = ids_col == ids_row
    lower = same & (row >= col)
    strict = same & (row > col)
    sums = (row >= col).astype(F32).astype(BF16)
    fresh = (ids_col == before).astype(F32)
    last_id = ids_col[count - 1 :, :]
    tail = (ids_col == last_id).astype(F32)
    kept = (last_id == before).astype(F32)
    cumul_all = dot(sums, g_ref[...])
    head_lane = lax.broadcasted_iota(jnp.int32, beta_ref.shape, 1)
    eye = (
        lax.broadcasted_iota(jnp.int32, (width, width), 0)
        == lax.broadcasted_iota(jnp.int32, (width, width), 1)
    )
    for h in range(TOGETHER):
        here = slice(h * width, (h + 1) * width)
        head = pl.program_id(0) * TOGETHER + h
        strength = jnp.sum(jnp.where(head_lane == head, beta_ref[...], 0.0), axis=1, keepdims=True)
        cumul = cumul_all[:, here]
        total = cumul[count - 1 :, :]
        middle = total * 0.5
        up = jnp.exp(cumul - middle)
        kn = unit_rows(k_ref[:, here].astype(F32))
        qn = unit_rows(q_ref[:, here].astype(F32))
        kneg = kn * jnp.exp(middle - cumul)
        kpos = kn * up * strength
        qpos = qn * up
        half = jnp.exp(middle)
        products = dot3(halves(jnp.concatenate([kpos, qpos], axis=0)), halves(kneg), ((1,), (1,)))
        system = jnp.where(strict, products[:count], 0.0)
        scores = jnp.where(lower, products[count:], 0.0)
        right = jnp.concatenate(
            [strength * v_ref[:, here].astype(F32), kpos * (half * fresh)], axis=1
        )
        updates = solve(system, right, count)
        khat = kneg * (half * tail)
        left = halves(jnp.concatenate([khat.T, scores], axis=0))
        found = dot3(left, updates)
        b_ref[h] = found[:width, :width]
        a_ref[h] = jnp.where(eye, jnp.exp(total) * kept, 0.0) - found[:width, width:]
        out_ref[:, here] = found[width:, :width]
        reach_ref[:, here] = qpos * (half * fresh) - found[width:, width:]


def span(lengths, queries, keys, values, beta, log_decay):
    count, total = queries.shape
    heads = beta.shape[1]
    width = total // heads
    cols = TOGETHER * width
    rows = pl.BlockSpec((count, cols), lambda i: (0, i))
    squares = pl.BlockSpec((TOGETHER, width, width), lambda i: (i, 0, 0))
    return pl.pallas_call(
        span_kernel,
        grid=(heads // TOGETHER,),
        in_specs=[
            pl.BlockSpec(memory_space=pltpu.SMEM),
            rows,
            rows,
            rows,
            pl.BlockSpec(beta.shape, lambda i: (0, 0)),
            rows,
        ],
        out_specs=[squares, squares, rows, rows],
        out_shape=[
            jax.ShapeDtypeStruct((heads, width, width), F32),
            jax.ShapeDtypeStruct((heads, width, width), F32),
            jax.ShapeDtypeStruct((count, total), F32),
            jax.ShapeDtypeStruct((count, total), F32),
        ],
        compiler_params=pltpu.CompilerParams(vmem_limit_bytes=48 << 20),
        name="span",
    )(lengths, queries, keys, values, beta, log_decay)


def pass_kernel(a_ref, b_ref, state_ref, out_ref):
    for h in range(a_ref.shape[0]):
        out_ref[h] = b_ref[h] + dot3(halves(a_ref[h]), halves(state_ref[h]))


def passed(trans_a, trans_b, state):
    heads, width, _ = trans_a.shape
    squares = pl.BlockSpec((4, width, width), lambda i: (i, 0, 0))
    return pl.pallas_call(
        pass_kernel,
        grid=(heads // 4,),
        in_specs=[squares] * 3,
        out_specs=squares,
        out_shape=jax.ShapeDtypeStruct(trans_a.shape, F32),
        name="pass_on",
    )(trans_a, trans_b, state)


def finish_kernel(out_ref, reach_ref, state_ref, gain_ref, mixed_ref):
    width = state_ref.shape[1]
    for h in range(state_ref.shape[0]):
        here = slice(h * width, (h + 1) * width)
        outs = out_ref[:, here] + dot3(halves(reach_ref[:, here]), halves(state_ref[h]))
        scale = lax.rsqrt(jnp.mean(outs * outs, axis=-1, keepdims=True) + 1e-06)
        mixed_ref[:, here] = (outs * scale * gain_ref[:, here]).astype(BF16)


def finished(outs, reach, state, gain):
    count, total = outs.shape
    heads, width, _ = state.shape
    rows = pl.BlockSpec((count, 4 * width), lambda i: (0, i))
    return pl.pallas_call(
        finish_kernel,
        grid=(heads // 4,),
        in_specs=[
            rows,
            rows,
            pl.BlockSpec((4, width, width), lambda i: (i, 0, 0)),
            pl.BlockSpec((1, 4 * width), lambda i: (0, i)),
        ],
        out_specs=rows,
        out_shape=jax.ShapeDtypeStruct((count, total), BF16),
        name="finish",
    )(outs, reach, state, gain)


def local(queries, keys, values, beta, log_decay, out_gain, doc_lengths):
    devices = lax.axis_size("ctx")
    pairs = [(i, i + 1) for i in range(devices - 1)]
    trans_a, trans_b, outs, reach = span(doc_lengths, queries, keys, values, beta, log_decay)
    state = lax.ppermute(trans_b, "ctx", pairs)
    for _ in range(devices // 2 - 1):
        state = lax.ppermute(passed(trans_a, trans_b, state), "ctx", pairs)
    return finished(outs, reach, state, out_gain.reshape(1, -1))


def solution(mesh):
    rows = P(("dp", "ctx"), None)
    return jax.shard_map(
        local,
        mesh=mesh,
        in_specs=(rows, rows, rows, rows, rows, P(), P("dp")),
        out_specs=rows,
        check_vma=False,
    )
```

```python
import functools

import jax
import jax.numpy as jnp
from jax import lax
from jax.experimental import pallas as pl
from jax.experimental.pallas import tpu as pltpu
from jax.sharding import PartitionSpec as P

F32 = jnp.float32
BF16 = jnp.bfloat16
TILE = 16
BLOCK = 64
GROUP = 4
LAG = 2


def halves(x):
    high = x.astype(BF16)
    return high, (x - high.astype(F32)).astype(BF16)


def dot(a, b, dims=((1,), (0,))):
    return lax.dot_general(a, b, (dims, ((), ())), preferred_element_type=F32)


def dot3(a, b, dims=((1,), (0,))):
    return dot(a[0], b[0], dims) + (dot(a[0], b[1], dims) + dot(a[1], b[0], dims))


def rows_of(pair, low, high):
    return pair[0][low:high], pair[1][low:high]


def unit_rows(x):
    return x * lax.rsqrt(jnp.sum(x * x, axis=-1, keepdims=True) + 1e-06)


def doc_ids(lengths_ref, first, shape, dim):
    place = first + lax.broadcasted_iota(jnp.int32, shape, dim)
    ids = jnp.zeros(shape, jnp.int32)
    before = jnp.int32(0)
    start = jnp.int32(0)
    for d in range(lengths_ref.shape[0]):
        ids = ids + (place >= start).astype(jnp.int32)
        before = before + (first > start).astype(jnp.int32)
        start = start + lengths_ref[d]
    return ids, before


def lanes_of(shape):
    return lax.broadcasted_iota(jnp.int32, shape, 1)


def side_by_side(system, count, size):
    lane = lanes_of((size, count)) // size
    side = system[:size]
    for b in range(1, count // size):
        side = jnp.where(lane == b, system[b * size : (b + 1) * size], side)
    return side


def tile_inverses(systems, count):
    sides = [side_by_side(s, count, TILE) for s in systems]
    whole = count // 128 * 128
    pieces = [s[:, low : low + 128] for s in sides for low in range(0, whole, 128)]
    rest = [s[:, whole:] for s in sides]
    if count > whole:
        for i in range(0, len(rest), 128 // (count - whole)):
            group = rest[i : i + 128 // (count - whole)]
            wide = sum(x.shape[1] for x in group)
            if wide < 128:
                group = group + [jnp.zeros((TILE, 128 - wide), F32)]
            pieces.append(jnp.concatenate(group, axis=1))
    lane = lanes_of((TILE, 128))
    home = lane - lane % TILE
    eye = (lane % TILE == lax.broadcasted_iota(jnp.int32, (TILE, 128), 0)).astype(F32)
    found = [[eye[8 * i : 8 * i + 8] for i in range(TILE // 8)] for _ in pieces]
    for j in range(TILE - 1):
        for p, piece in enumerate(pieces):
            line = found[p][j // 8][j % 8 : j % 8 + 1, :]
            for i in range((j + 1) // 8, TILE // 8):
                column = jnp.take_along_axis(
                    piece[8 * i : 8 * i + 8], home[:8] + j, axis=1, mode="promise_in_bounds"
                )
                found[p][i] = found[p][i] - column * line
    found = [jnp.concatenate(x, axis=0) for x in found]
    each = whole // 128
    results = []
    for h in range(len(systems)):
        parts = found[h * each : (h + 1) * each]
        if count > whole:
            per = 128 // (count - whole)
            at = h % per * (count - whole)
            parts = parts + [found[each * len(systems) + h // per][:, at : at + count - whole]]
        results.append(jnp.concatenate(parts, axis=1))
    return results


def spread(side, count, height, column_of):
    block = column_of(lanes_of(side.shape) // height)
    return jnp.concatenate([jnp.where(block == b, side, 0.0) for b in range(count // height)], axis=0)


def merged(system, side, count, size):
    lane = lanes_of(side.shape) // size
    even = lane % 2 == 0
    below = jnp.zeros(side.shape, F32)
    for b in range(1, count // size, 2):
        below = jnp.where(lane == b - 1, system[b * size : (b + 1) * size, :], below)
    wide = spread(side, count, size, lambda x: x)
    middle = dot3(halves(below), halves(wide))
    tall = spread(middle, count, size, lambda x: jnp.where(x % 2 == 0, x + 1, -1))
    corner = dot3(halves(jnp.where(even, 0.0, side)), halves(tall))
    return jnp.concatenate([jnp.where(even, side, 0.0), jnp.where(even, -corner, side)], axis=0)


def solve(systems, rights, count):
    sides = tile_inverses(systems, count)
    size = TILE
    while size < BLOCK:
        sides = [merged(s, x, count, size) for s, x in zip(systems, sides)]
        size = 2 * size
    wides = [halves(spread(x, count, BLOCK, lambda x: x)) for x in sides]
    row = lax.broadcasted_iota(jnp.int32, (count, count), 0) // BLOCK
    outside = row > lanes_of((count, count)) // BLOCK
    splits = [halves(jnp.where(outside, s, 0.0)) for s in systems]
    firsts = [dot3(w, r) for w, r in zip(wides, rights)]
    links = [halves(dot3(rows_of(w, BLOCK, count), s)) for w, s in zip(wides, splits)]
    done = [halves(x[:BLOCK]) for x in firsts]
    for b in range(1, count // BLOCK):
        low, high = b * BLOCK, (b + 1) * BLOCK
        for h in range(len(systems)):
            link = tuple(x[low - BLOCK : low, :low] for x in links[h])
            part = halves(firsts[h][low:high] - dot3(link, done[h]))
            done[h] = tuple(jnp.concatenate(x, axis=0) for x in zip(done[h], part))
    return done


def span_kernel(
    group, lengths_ref, q_ref, k_ref, v_ref, beta_ref, g_ref, a_ref, b_ref, out_ref, reach_ref
):
    count = q_ref.shape[0]
    width = a_ref.shape[1]
    first = lax.axis_index("ctx") * count
    ids_col, before = doc_ids(lengths_ref, first, (count, 1), 0)
    ids_row, _ = doc_ids(lengths_ref, first, (1, count), 1)
    row = lax.broadcasted_iota(jnp.int32, (count, count), 0)
    col = lanes_of((count, count))
    same = ids_col == ids_row
    lower = same & (row >= col)
    strict = same & (row > col)
    sums = (row >= col).astype(F32).astype(BF16)
    fresh = ids_col == before
    tail = (ids_row == ids_row[:, count - 1 :]).astype(F32)
    kept = (ids_row[:, count - 1 :] == before).astype(F32)
    cumul_all = dot(sums, g_ref[...])
    eye = lax.broadcasted_iota(jnp.int32, (width, width), 0) == lanes_of((width, width))
    heads = range(a_ref.shape[0])
    here = [slice(h * width, (h + 1) * width) for h in heads]
    strength = [beta_ref[group * len(heads) + h :][:1] for h in heads]
    total, half, kneg, kpos, qpos = [], [], [], [], []
    for h in heads:
        cumul = cumul_all[:, here[h]]
        total.append(cumul[count - 1 :, :])
        middle = total[h] * 0.5
        half.append(jnp.exp(middle))
        up = jnp.exp(cumul - middle)
        kn = unit_rows(k_ref[:, here[h]].astype(F32))
        kneg.append(kn * jnp.exp(middle - cumul))
        kpos.append(kn * up)
        qpos.append(unit_rows(q_ref[:, here[h]].astype(F32)) * up)
    products = [
        dot3(halves(jnp.concatenate([kpos[h], qpos[h]], axis=0)), halves(kneg[h]), ((1,), (1,)))
        * strength[h]
        for h in heads
    ]
    systems = [jnp.where(strict, x[:count], 0.0) for x in products]
    rights = []
    for h in heads:
        high, low = halves(kpos[h] * half[h])
        value = v_ref[:, here[h]]
        rights.append(
            (
                jnp.concatenate([value, high], axis=1),
                jnp.concatenate([jnp.zeros_like(value), low], axis=1),
            )
        )
    updates = solve(systems, rights, count)
    for h in heads:
        scores = jnp.where(lower, products[h][count:], 0.0)
        khat = (kneg[h] * half[h]).T * (strength[h] * tail)
        found = dot3(halves(jnp.concatenate([khat, scores], axis=0)), updates[h])
        b_ref[h] = found[:width, :width]
        a_ref[h] = (jnp.where(eye, jnp.exp(total[h]), 0.0) - found[:width, width:]) * kept
        out_ref[:, here[h]] = found[width:, :width]
        reach_ref[:, here[h]] = jnp.where(fresh, qpos[h] * half[h] - found[width:, width:], 0.0)


VMEM = pl.BlockSpec(memory_space=pltpu.VMEM)
SMEM = pl.BlockSpec(memory_space=pltpu.SMEM)


def span(group, lengths, queries, keys, values, strength, log_decay):
    count, total = queries.shape
    heads = strength.shape[0]
    width = total // heads
    cols = GROUP * width
    rows = pl.BlockSpec((count, cols), lambda i: (0, group))
    square = jax.ShapeDtypeStruct((GROUP, width, width), F32)
    part = jax.ShapeDtypeStruct((count, cols), F32)
    return pl.pallas_call(
        functools.partial(span_kernel, group),
        grid=(1,),
        in_specs=[SMEM, rows, rows, rows, VMEM, rows],
        out_specs=[VMEM] * 4,
        out_shape=[square, square, part, part],
        compiler_params=pltpu.CompilerParams(vmem_limit_bytes=32 << 20),
        name="span",
    )(lengths, queries, keys, values, strength, log_decay)


def spans_back(lengths_ref, count, most):
    first = lax.axis_index("ctx") * count
    start = jnp.int32(0)
    latest = jnp.int32(0)
    fresh = jnp.int32(0)
    for d in range(lengths_ref.shape[0]):
        latest = jnp.where(start < first, start, latest)
        fresh = jnp.where((start >= first) & (start < first + count), 1, fresh)
        start = start + lengths_ref[d]
    back = jnp.int32(0)
    for i in range(1, most):
        back = back + jnp.where(latest < first - i * count, 1, 0)
    return back, fresh


def pass_kernel(count, most, own, low, late, lengths_ref, state_ref, *refs):
    out_ref = refs[-1]
    before, fresh = spans_back(lengths_ref, count, most)
    for h in range(out_ref.shape[0]):
        trans_a, trans_b = refs[own][h], refs[own + 1][h]
        for i in range(1, late):
            here = before == low + i
            trans_a = jnp.where(here, refs[own + 2 * i][h], trans_a)
            trans_b = jnp.where(here, refs[own + 2 * i + 1][h], trans_b)
        sent = trans_b + dot3(halves(trans_a), halves(state_ref[h]))
        out_ref[h] = jnp.where(fresh == 1, refs[0][h], sent) if own else sent


def message(step, count, most, lengths, trans_a, trans_b, received):
    own = [trans_b[step]] if step < len(trans_b) else []
    if step < LAG:
        return own[0]
    late = [step - LAG * i for i in range(1, most)]
    low = next(i for i, x in enumerate(late) if x < len(trans_b))
    late = [x for x in late if 0 <= x < len(trans_b)]
    carried = [x for g in late for x in (trans_a[g], trans_b[g])]
    return pl.pallas_call(
        functools.partial(pass_kernel, count, most, len(own), low, len(late)),
        in_specs=[SMEM] + [VMEM] * (1 + len(own) + len(carried)),
        out_specs=VMEM,
        out_shape=jax.ShapeDtypeStruct(trans_b[0].shape, F32),
        compiler_params=pltpu.CompilerParams(vmem_limit_bytes=8 << 20),
        name="pass_on",
    )(lengths, received[step - LAG], *own, *carried)


def finish_kernel(lengths_ref, out_ref, reach_ref, gain_ref, *refs):
    states = refs[:-2]
    mixed_ref = refs[-1]
    heads, width, _ = states[0].shape
    before, _ = spans_back(lengths_ref, out_ref.shape[0], len(states))
    for h in range(heads):
        here = slice(h * width, (h + 1) * width)
        state = states[0][h]
        for i in range(1, len(states)):
            state = jnp.where(before == i, states[i][h], state)
        outs = out_ref[:, here] + dot3(halves(reach_ref[:, here]), halves(state))
        scale = lax.rsqrt(jnp.mean(outs * outs, axis=-1, keepdims=True) + 1e-06)
        mixed_ref[:, here] = (outs * scale * gain_ref[:, here]).astype(BF16)


def finished(group, mixed, lengths, outs, reach, states, gain):
    count, cols = outs.shape
    return pl.pallas_call(
        finish_kernel,
        grid=(1,),
        in_specs=[SMEM, VMEM, VMEM, pl.BlockSpec((1, cols), lambda i: (0, group))]
        + [VMEM] * len(states)
        + [pl.BlockSpec(memory_space=pl.ANY)],
        out_specs=pl.BlockSpec((count, cols), lambda i: (0, group)),
        out_shape=jax.ShapeDtypeStruct(mixed.shape, BF16),
        input_output_aliases={4 + len(states): 0},
        compiler_params=pltpu.CompilerParams(vmem_limit_bytes=8 << 20),
        name="finish",
    )(lengths, outs, reach, gain, *states, mixed)


def local(queries, keys, values, beta, log_decay, out_gain, doc_lengths):
    devices = lax.axis_size("ctx")
    pairs = [(i, i + 1) for i in range(devices - 1)]
    count = queries.shape[0]
    groups = beta.shape[1] // GROUP
    most = devices // 2
    queries, keys, values, log_decay = (
        pltpu.with_memory_space_constraint(x, pltpu.HBM)
        for x in (queries, keys, values, log_decay)
    )
    strength = beta.T
    trans_a, trans_b, outs, reach = zip(
        *(
            span(g, doc_lengths, queries, keys, values, strength, log_decay)
            for g in range(groups)
        )
    )
    received = []
    for step in range(groups + LAG * (most - 1)):
        sent = message(step, count, most, doc_lengths, trans_a, trans_b, received)
        received.append(lax.ppermute(sent, "ctx", pairs))
    mixed = jnp.zeros(queries.shape, BF16)
    gain = out_gain.reshape(1, -1)
    for g in range(groups):
        states = [received[g + LAG * i] for i in range(most)]
        mixed = finished(g, mixed, doc_lengths, outs[g], reach[g], states, gain)
    return mixed


def solution(mesh):
    rows = P(("dp", "ctx"), None)
    return jax.shard_map(
        local,
        mesh=mesh,
        in_specs=(rows, rows, rows, rows, rows, P(), P("dp")),
        out_specs=rows,
        check_vma=False,
    )
```

```python
import functools

import jax
import jax.numpy as jnp
from jax import lax
from jax.experimental import pallas as pl
from jax.experimental.pallas import tpu as pltpu
from jax.sharding import PartitionSpec as P

F32 = jnp.float32
BF16 = jnp.bfloat16
TILE = 16
BLOCK = 64
SPAN = 4
GROUP = 4
LAG = 2
FINISH = 4
AHEAD = 0
COST = pl.CostEstimate(flops=1, transcendentals=0, bytes_accessed=1)


def halves(x):
    high = x.astype(BF16)
    return high, (x - high.astype(F32)).astype(BF16)


def dot(a, b, dims=((1,), (0,))):
    return lax.dot_general(a, b, (dims, ((), ())), preferred_element_type=F32)


def dot3(a, b, dims=((1,), (0,))):
    return dot(a[0], b[0], dims) + (dot(a[0], b[1], dims) + dot(a[1], b[0], dims))


def rows_of(pair, low, high):
    return pair[0][low:high], pair[1][low:high]


def unit_rows(x):
    return x * lax.rsqrt(jnp.sum(x * x, axis=-1, keepdims=True) + 1e-06)


def doc_ids(lengths_ref, first, shape, dim):
    place = first + lax.broadcasted_iota(jnp.int32, shape, dim)
    ids = jnp.zeros(shape, jnp.int32)
    before = jnp.int32(0)
    start = jnp.int32(0)
    for d in range(lengths_ref.shape[0]):
        ids = ids + (place >= start).astype(jnp.int32)
        before = before + (first > start).astype(jnp.int32)
        start = start + lengths_ref[d]
    return ids, before


def lanes_of(shape):
    return lax.broadcasted_iota(jnp.int32, shape, 1)


def side_by_side(system, count, size):
    lane = lanes_of((size, count)) // size
    side = system[:size]
    for b in range(1, count // size):
        side = jnp.where(lane == b, system[b * size : (b + 1) * size], side)
    return side


def tile_inverses(systems, count):
    sides = [side_by_side(s, count, TILE) for s in systems]
    whole = count // 128 * 128
    pieces = [s[:, low : low + 128] for s in sides for low in range(0, whole, 128)]
    rest = [s[:, whole:] for s in sides]
    if count > whole:
        for i in range(0, len(rest), 128 // (count - whole)):
            group = rest[i : i + 128 // (count - whole)]
            wide = sum(x.shape[1] for x in group)
            if wide < 128:
                group = group + [jnp.zeros((TILE, 128 - wide), F32)]
            pieces.append(jnp.concatenate(group, axis=1))
    lane = lanes_of((TILE, 128))
    home = lane - lane % TILE
    eye = (lane % TILE == lax.broadcasted_iota(jnp.int32, (TILE, 128), 0)).astype(F32)
    found = [[eye[8 * i : 8 * i + 8] for i in range(TILE // 8)] for _ in pieces]
    for j in range(TILE - 1):
        for p, piece in enumerate(pieces):
            line = found[p][j // 8][j % 8 : j % 8 + 1, :]
            for i in range((j + 1) // 8, TILE // 8):
                column = jnp.take_along_axis(
                    piece[8 * i : 8 * i + 8], home[:8] + j, axis=1, mode="promise_in_bounds"
                )
                found[p][i] = found[p][i] - column * line
    found = [jnp.concatenate(x, axis=0) for x in found]
    each = whole // 128
    results = []
    for h in range(len(systems)):
        parts = found[h * each : (h + 1) * each]
        if count > whole:
            per = 128 // (count - whole)
            at = h % per * (count - whole)
            parts = parts + [found[each * len(systems) + h // per][:, at : at + count - whole]]
        results.append(jnp.concatenate(parts, axis=1))
    return results


def spread(side, count, height, column_of):
    block = column_of(lanes_of(side.shape) // height)
    return jnp.concatenate([jnp.where(block == b, side, 0.0) for b in range(count // height)], axis=0)


def merged(system, side, count, size):
    lane = lanes_of(side.shape) // size
    even = lane % 2 == 0
    below = jnp.zeros(side.shape, F32)
    for b in range(1, count // size, 2):
        below = jnp.where(lane == b - 1, system[b * size : (b + 1) * size, :], below)
    wide = spread(side, count, size, lambda x: x)
    middle = dot3(halves(below), halves(wide))
    tall = spread(middle, count, size, lambda x: jnp.where(x % 2 == 0, x + 1, -1))
    corner = dot3(halves(jnp.where(even, 0.0, side)), halves(tall))
    return jnp.concatenate([jnp.where(even, side, 0.0), jnp.where(even, -corner, side)], axis=0)


def solve(systems, rights, count):
    sides = tile_inverses(systems, count)
    size = TILE
    while size < BLOCK:
        sides = [merged(s, x, count, size) for s, x in zip(systems, sides)]
        size = 2 * size
    wides = [halves(spread(x, count, BLOCK, lambda x: x)) for x in sides]
    row = lax.broadcasted_iota(jnp.int32, (count, count), 0) // BLOCK
    outside = row > lanes_of((count, count)) // BLOCK
    splits = [halves(jnp.where(outside, s, 0.0)) for s in systems]
    firsts = [dot3(w, r) for w, r in zip(wides, rights)]
    links = [halves(dot3(rows_of(w, BLOCK, count), s)) for w, s in zip(wides, splits)]
    done = [halves(x[:BLOCK]) for x in firsts]
    for b in range(1, count // BLOCK):
        low, high = b * BLOCK, (b + 1) * BLOCK
        for h in range(len(systems)):
            link = tuple(x[low - BLOCK : low, :low] for x in links[h])
            part = halves(firsts[h][low:high] - dot3(link, done[h]))
            done[h] = tuple(jnp.concatenate(x, axis=0) for x in zip(done[h], part))
    return done


def documents(lengths_ref, count, most, strict_ref, lower_ref, fresh_ref, flags_ref):
    first = lax.axis_index("ctx") * count
    ids_col, before = doc_ids(lengths_ref, first, (count, 1), 0)
    ids_row, _ = doc_ids(lengths_ref, first, (1, count), 1)
    row = lax.broadcasted_iota(jnp.int32, (count, count), 0)
    col = lanes_of((count, count))
    same = ids_col == ids_row
    lower_ref[...] = (same & (row >= col)).astype(F32)
    strict_ref[...] = (same & (row > col)).astype(F32)
    fresh_ref[...] = jnp.broadcast_to((ids_col == before).astype(F32), fresh_ref.shape)
    last = ids_row[:, count - 1 :]
    start = jnp.int32(0)
    latest = jnp.int32(0)
    for d in range(lengths_ref.shape[0]):
        latest = jnp.where(start < first, start, latest)
        start = start + lengths_ref[d]
    back = jnp.int32(0)
    for i in range(1, most):
        back = back + jnp.where(latest < first - i * count, 1, 0)
    flags_ref[0:1, :] = (ids_row == last).astype(F32)
    flags_ref[1:2, :] = jnp.broadcast_to((last == before).astype(F32), (1, count))
    flags_ref[2:3, :] = jnp.full((1, count), back.astype(F32))


def span_heads(head, q_ref, k_ref, v_ref, beta_ref, g_ref, strict_ref, lower_ref, fresh_ref, flags_ref, refs):
    count = q_ref.shape[0]
    out_ref, reach_ref = refs[0], refs[1]
    a_refs, b_refs = refs[2::2], refs[3::2]
    group, width, _ = a_refs[0].shape
    heads = range(len(a_refs) * group)
    here = [slice((head + h) * width, (head + h + 1) * width) for h in heads]
    row = lax.broadcasted_iota(jnp.int32, (count, count), 0)
    sums = (row >= lanes_of((count, count))).astype(F32).astype(BF16)
    cumul_all = dot(sums, g_ref[:, here[0].start : here[-1].stop])
    eye = lax.broadcasted_iota(jnp.int32, (width, width), 0) == lanes_of((width, width))
    strength = [beta_ref[head + h : head + h + 1, :] for h in heads]
    tail = flags_ref[0:1, :]
    kept = flags_ref[1:2, :width]
    total, half, kneg, kpos, qpos = [], [], [], [], []
    for h in heads:
        cumul = cumul_all[:, h * width : (h + 1) * width]
        total.append(cumul[count - 1 :, :])
        middle = total[h] * 0.5
        half.append(jnp.exp(middle))
        up = jnp.exp(cumul - middle)
        kn = unit_rows(k_ref[:, here[h]].astype(F32))
        kneg.append(kn * jnp.exp(middle - cumul))
        kpos.append(kn * up)
        qpos.append(unit_rows(q_ref[:, here[h]].astype(F32)) * up)
    products = [
        dot3(halves(jnp.concatenate([kpos[h], qpos[h]], axis=0)), halves(kneg[h]), ((1,), (1,)))
        * strength[h]
        for h in heads
    ]
    strict = strict_ref[...] > 0.0
    systems = [jnp.where(strict, x[:count], 0.0) for x in products]
    rights = []
    for h in heads:
        high, low = halves(kpos[h] * half[h])
        value = v_ref[:, here[h]]
        rights.append(
            (
                jnp.concatenate([value, high], axis=1),
                jnp.concatenate([jnp.zeros_like(value), low], axis=1),
            )
        )
    updates = solve(systems, rights, count)
    lower = lower_ref[...] > 0.0
    fresh = fresh_ref[...] > 0.0
    for h in heads:
        scores = jnp.where(lower, products[h][count:], 0.0)
        khat = (kneg[h] * half[h]).T * (strength[h] * tail)
        found = dot3(halves(jnp.concatenate([khat, scores], axis=0)), updates[h])
        b_refs[h // group][h % group] = found[:width, :width]
        a_refs[h // group][h % group] = (
            jnp.where(eye, jnp.exp(total[h]), 0.0) - found[:width, width:]
        ) * kept
        at = slice(h * width, (h + 1) * width)
        out_ref[:, at] = found[width:, :width]
        reach_ref[:, at] = jnp.where(fresh, qpos[h] * half[h] - found[width:, width:], 0.0)


VMEM = pl.BlockSpec(memory_space=pltpu.VMEM)
ANY = pl.BlockSpec(memory_space=pl.ANY)


def opening_kernel(most, *refs):
    lengths_hbm, beta_hbm, *sources = refs[:6]
    beta_ref, *targets = refs[6:11]
    masks = refs[11:15]
    outs = refs[15:-2]
    lengths_ref, sems = refs[-2:]
    count = sources[0].shape[0]
    cols = outs[0].shape[1]
    first = [(lengths_hbm, lengths_ref), (beta_hbm, beta_ref)]
    first += [(x.at[:, :cols], y.at[:, :cols]) for x, y in zip(sources, targets)]
    rest = [(x.at[:, cols:], y.at[:, cols:]) for x, y in zip(sources, targets)]
    copies = [pltpu.make_async_copy(x, y, sems.at[i]) for i, (x, y) in enumerate(first + rest)]
    for copy in copies:
        copy.start()
    copies[0].wait()
    documents(lengths_ref, count, most, *masks)
    for copy in copies[1 : len(first)]:
        copy.wait()
    q_ref, k_ref, v_ref, g_ref = targets
    span_heads(0, q_ref, k_ref, v_ref, beta_ref, g_ref, *masks, outs)
    for copy in copies[len(first) :]:
        copy.wait()


def span_shapes(count, width):
    part = jax.ShapeDtypeStruct((count, SPAN * width), F32)
    square = jax.ShapeDtypeStruct((GROUP, width, width), F32)
    return [part, part] + [square] * (2 * SPAN // GROUP)


def opening(most, lengths, strength, queries, keys, values, log_decay):
    count, total = queries.shape
    heads = strength.shape[0]
    width = total // heads
    given = [lengths, strength, queries, keys, values, log_decay]
    given = [pltpu.with_memory_space_constraint(x, pltpu.HBM) for x in given]
    square = jax.ShapeDtypeStruct((count, count), F32)
    kept = [jax.ShapeDtypeStruct(x.shape, x.dtype) for x in given[1:]]
    kept += [
        square,
        square,
        jax.ShapeDtypeStruct((count, width), F32),
        jax.ShapeDtypeStruct((8, count), F32),
    ]
    shapes = kept + span_shapes(count, width)
    results = pl.pallas_call(
        functools.partial(opening_kernel, most),
        in_specs=[ANY] * len(given),
        out_specs=[VMEM] * len(shapes),
        out_shape=shapes,
        scratch_shapes=[pltpu.SMEM(lengths.shape, lengths.dtype), pltpu.SemaphoreType.DMA((10,))],
        compiler_params=pltpu.CompilerParams(vmem_limit_bytes=32 << 20),
        cost_estimate=COST,
        name="opening",
    )(*given)
    return results[: len(kept)], results[len(kept) :]


def span_kernel(head, beta_ref, q_ref, k_ref, v_ref, g_ref, *refs):
    span_heads(head, q_ref, k_ref, v_ref, beta_ref, g_ref, *refs[:4], refs[4:])


def span(head, shared):
    count = shared[1].shape[0]
    width = shared[1].shape[1] // shared[0].shape[0]
    shapes = span_shapes(count, width)
    return pl.pallas_call(
        functools.partial(span_kernel, head),
        in_specs=[VMEM] * len(shared),
        out_specs=[VMEM] * len(shapes),
        out_shape=shapes,
        compiler_params=pltpu.CompilerParams(vmem_limit_bytes=32 << 20),
        cost_estimate=COST,
        name="span",
    )(*shared)


def pass_kernel(own, low, late, flags_ref, state_ref, *refs):
    out_ref = refs[-1]
    width = out_ref.shape[1]
    before = flags_ref[2:3, :width]
    for h in range(out_ref.shape[0]):
        trans_a, trans_b = refs[own][h], refs[own + 1][h]
        for i in range(1, late):
            here = before == low + i
            trans_a = jnp.where(here, refs[own + 2 * i][h], trans_a)
            trans_b = jnp.where(here, refs[own + 2 * i + 1][h], trans_b)
        sent = trans_b + dot3(halves(trans_a), halves(state_ref[h]))
        out_ref[h] = jnp.where(flags_ref[1:2, :width] > 0.0, sent, refs[0][h]) if own else sent


def message(step, most, flags, trans_a, trans_b, received):
    own = [trans_b[step]] if step < len(trans_b) else []
    if step < LAG:
        return own[0]
    late = [step - LAG * i for i in range(1, most)]
    low = next(i for i, x in enumerate(late) if x < len(trans_b))
    late = [x for x in late if 0 <= x < len(trans_b)]
    carried = [x for g in late for x in (trans_a[g], trans_b[g])]
    return pl.pallas_call(
        functools.partial(pass_kernel, len(own), low, len(late)),
        in_specs=[VMEM] * (2 + len(own) + len(carried)),
        out_specs=VMEM,
        out_shape=jax.ShapeDtypeStruct(trans_b[0].shape, F32),
        compiler_params=pltpu.CompilerParams(vmem_limit_bytes=8 << 20),
        cost_estimate=COST,
        name="pass_on",
    )(flags, received[step - LAG], *own, *carried)


def finish_kernel(head, most, spans, flags_ref, gain_ref, *refs):
    mixed_ref = refs[-1]
    outs, reach = refs[:spans], refs[spans : 2 * spans]
    states = refs[2 * spans : -1]
    group, width, _ = states[0].shape
    before = flags_ref[2:3, :width]
    for h in range(mixed_ref.shape[1] // width):
        at = (head + h) % SPAN * width
        here = slice(at, at + width)
        state = states[h // group * most][h % group]
        for i in range(1, most):
            state = jnp.where(before == i, states[h // group * most + i][h % group], state)
        of = h // SPAN
        total = outs[of][:, here] + dot3(halves(reach[of][:, here]), halves(state))
        scale = lax.rsqrt(jnp.mean(total * total, axis=-1, keepdims=True) + 1e-06)
        gain = gain_ref[:, (head + h) * width : (head + h + 1) * width]
        mixed_ref[:, h * width : (h + 1) * width] = (total * scale * gain).astype(BF16)


def finish_first(*refs):
    finish_kernel(*refs)


def finish_next(head, most, spans, flags_ref, gain_ref, *refs):
    finish_kernel(head, most, spans, flags_ref, gain_ref, *refs[:-2], refs[-1])


def finished(head, mixed, flags, outs, reach, received, most, gain):
    count = outs[0].shape[0]
    width = received[0].shape[1]
    low, high = head // SPAN, (head + FINISH - 1) // SPAN + 1
    groups = range(head // GROUP, (head + FINISH) // GROUP)
    states = [received[g + LAG * i] for g in groups for i in range(most)]
    given = [flags, gain, *outs[low:high], *reach[low:high], *states]
    specs = [VMEM] * len(given)
    aliases = {}
    if mixed is not None:
        aliases = {len(given): 0}
        given.append(mixed)
        specs.append(ANY)
    kernel = finish_first if mixed is None else finish_next
    return pl.pallas_call(
        functools.partial(kernel, head, most, high - low),
        grid=(1,),
        in_specs=specs,
        out_specs=pl.BlockSpec((count, FINISH * width), lambda i: (0, head // FINISH)),
        out_shape=jax.ShapeDtypeStruct((count, gain.shape[1]), BF16),
        input_output_aliases=aliases,
        compiler_params=pltpu.CompilerParams(vmem_limit_bytes=8 << 20),
        cost_estimate=COST,
        name="finish",
    )(*given)


def then(flags, results):
    flags, results = lax.optimization_barrier((flags, tuple(results)))
    return flags, list(results)


def local(queries, keys, values, beta, log_decay, out_gain, doc_lengths):
    devices = lax.axis_size("ctx")
    ring = [(i, (i + 1) % devices) for i in range(devices)]
    heads = beta.shape[1]
    most = devices // 2
    shared, first = opening(most, doc_lengths, beta.T, queries, keys, values, log_decay)
    shared, flags = shared[:-1], shared[-1]
    flags, first = then(flags, first)
    outs, reach, trans_a, trans_b, received = [], [], [], [], []
    mixed = None
    gain = out_gain.reshape(1, -1)
    groups = heads // GROUP
    steps = groups + LAG * (most - 1)
    head = SPAN

    def keep(found):
        outs.append(found[0])
        reach.append(found[1])
        trans_a.extend(found[2::2])
        trans_b.extend(found[3::2])

    keep(first)
    ended = 0
    for step in range(steps):
        while head < heads and head < (step + 1 + AHEAD * (step >= LAG)) * GROUP:
            flags, found = then(flags, span(head, [*shared, flags]))
            keep(found)
            head += SPAN
        sent = message(step, most, flags, trans_a, trans_b, received)
        if step >= LAG:
            flags, (sent,) = then(flags, [sent])
        received.append(lax.ppermute(sent, "ctx", ring))
        while head >= heads and ended + FINISH <= (step - 1 - LAG * (most - 1)) * GROUP:
            mixed = finished(ended, mixed, flags, outs, reach, received, most, gain)
            flags, (mixed,) = then(flags, [mixed])
            ended += FINISH
    for h in range(ended, heads, FINISH):
        mixed = finished(h, mixed, flags, outs, reach, received, most, gain)
    return mixed


def solution(mesh):
    rows = P(("dp", "ctx"), None)
    return jax.shard_map(
        local,
        mesh=mesh,
        in_specs=(rows, rows, rows, rows, rows, P(), P("dp")),
        out_specs=rows,
        check_vma=False,
    )
```

```python
import functools

import jax
import jax.numpy as jnp
from jax import lax
from jax.experimental import pallas as pl
from jax.experimental.pallas import tpu as pltpu
from jax.sharding import PartitionSpec as P

F32 = jnp.float32
BF16 = jnp.bfloat16
TILE = 16
BLOCK = 64
SPANS = ((2,), (2, 2), (2, 2), (2, 2), (2,))
LAG = 3
FILL = (1,) * 99
LATE = 2
QUERY = pl.CostEstimate(flops=10**8, transcendentals=0, bytes_accessed=1)
COST = pl.CostEstimate(flops=10**8, transcendentals=0, bytes_accessed=1)
PASS = pl.CostEstimate(flops=10**6, transcendentals=0, bytes_accessed=1)
END = pl.CostEstimate(flops=10**8, transcendentals=0, bytes_accessed=1)


def halves(x):
    high = x.astype(BF16)
    return high, (x - high.astype(F32)).astype(BF16)


def dot(a, b, dims=((1,), (0,))):
    return lax.dot_general(a, b, (dims, ((), ())), preferred_element_type=F32)


def dot3(a, b, dims=((1,), (0,))):
    return dot(a[0], b[0], dims) + (dot(a[0], b[1], dims) + dot(a[1], b[0], dims))


def rows_of(pair, low, high):
    return pair[0][low:high], pair[1][low:high]


def unit_rows(x):
    return x * lax.rsqrt(jnp.sum(x * x, axis=-1, keepdims=True) + 1e-06)


def doc_ids(lengths_ref, first, shape, dim):
    place = first + lax.broadcasted_iota(jnp.int32, shape, dim)
    ids = jnp.zeros(shape, jnp.int32)
    before = jnp.int32(0)
    start = jnp.int32(0)
    for d in range(lengths_ref.shape[0]):
        ids = ids + (place >= start).astype(jnp.int32)
        before = before + (first > start).astype(jnp.int32)
        start = start + lengths_ref[d]
    return ids, before


def lanes_of(shape):
    return lax.broadcasted_iota(jnp.int32, shape, 1)


def side_by_side(system, count, size):
    lane = lanes_of((size, count)) // size
    side = system[:size]
    for b in range(1, count // size):
        side = jnp.where(lane == b, system[b * size : (b + 1) * size], side)
    return side


def tile_inverses(systems, count):
    sides = [side_by_side(s, count, TILE) for s in systems]
    whole = count // 128 * 128
    pieces = [s[:, low : low + 128] for s in sides for low in range(0, whole, 128)]
    rest = [s[:, whole:] for s in sides]
    if count > whole:
        for i in range(0, len(rest), 128 // (count - whole)):
            group = rest[i : i + 128 // (count - whole)]
            wide = sum(x.shape[1] for x in group)
            if wide < 128:
                group = group + [jnp.zeros((TILE, 128 - wide), F32)]
            pieces.append(jnp.concatenate(group, axis=1))
    lane = lanes_of((TILE, 128))
    home = lane - lane % TILE
    eye = (lane % TILE == lax.broadcasted_iota(jnp.int32, (TILE, 128), 0)).astype(F32)
    found = [[eye[8 * i : 8 * i + 8] for i in range(TILE // 8)] for _ in pieces]
    for j in range(TILE - 1):
        for p, piece in enumerate(pieces):
            line = found[p][j // 8][j % 8 : j % 8 + 1, :]
            for i in range((j + 1) // 8, TILE // 8):
                column = jnp.take_along_axis(
                    piece[8 * i : 8 * i + 8], home[:8] + j, axis=1, mode="promise_in_bounds"
                )
                found[p][i] = found[p][i] - column * line
    found = [jnp.concatenate(x, axis=0) for x in found]
    each = whole // 128
    results = []
    for h in range(len(systems)):
        parts = found[h * each : (h + 1) * each]
        if count > whole:
            per = 128 // (count - whole)
            at = h % per * (count - whole)
            parts = parts + [found[each * len(systems) + h // per][:, at : at + count - whole]]
        results.append(jnp.concatenate(parts, axis=1))
    return results


def spread(side, count, height, column_of):
    block = column_of(lanes_of(side.shape) // height)
    return jnp.concatenate([jnp.where(block == b, side, 0.0) for b in range(count // height)], axis=0)


def merged(system, side, count, size):
    lane = lanes_of(side.shape) // size
    even = lane % 2 == 0
    below = jnp.zeros(side.shape, F32)
    for b in range(1, count // size, 2):
        below = jnp.where(lane == b - 1, system[b * size : (b + 1) * size, :], below)
    wide = spread(side, count, size, lambda x: x)
    middle = dot3(halves(below), halves(wide))
    tall = spread(middle, count, size, lambda x: jnp.where(x % 2 == 0, x + 1, -1))
    corner = dot3(halves(jnp.where(even, 0.0, side)), halves(tall))
    return jnp.concatenate([jnp.where(even, side, 0.0), jnp.where(even, -corner, side)], axis=0)


def solve(systems, rights, count):
    sides = tile_inverses(systems, count)
    size = TILE
    while size < BLOCK:
        sides = [merged(s, x, count, size) for s, x in zip(systems, sides)]
        size = 2 * size
    wides = [halves(spread(x, count, BLOCK, lambda x: x)) for x in sides]
    row = lax.broadcasted_iota(jnp.int32, (count, count), 0) // BLOCK
    outside = row > lanes_of((count, count)) // BLOCK
    splits = [halves(jnp.where(outside, s, 0.0)) for s in systems]
    firsts = [dot3(w, r) for w, r in zip(wides, rights)]
    links = [halves(dot3(rows_of(w, BLOCK, count), s)) for w, s in zip(wides, splits)]
    done = [halves(x[:BLOCK]) for x in firsts]
    for b in range(1, count // BLOCK):
        low, high = b * BLOCK, (b + 1) * BLOCK
        for h in range(len(systems)):
            link = tuple(x[low - BLOCK : low, :low] for x in links[h])
            part = halves(firsts[h][low:high] - dot3(link, done[h]))
            done[h] = tuple(jnp.concatenate(x, axis=0) for x in zip(done[h], part))
    return done


def documents(lengths_ref, count, most, strict_ref, lower_ref, fresh_ref, flags_ref):
    first = lax.axis_index("ctx") * count
    ids_col, before = doc_ids(lengths_ref, first, (count, 1), 0)
    ids_row, _ = doc_ids(lengths_ref, first, (1, count), 1)
    row = lax.broadcasted_iota(jnp.int32, (count, count), 0)
    col = lanes_of((count, count))
    same = ids_col == ids_row
    lower_ref[...] = (same & (row >= col)).astype(F32)
    strict_ref[...] = (same & (row > col)).astype(F32)
    fresh_ref[...] = jnp.broadcast_to((ids_col == before).astype(F32), fresh_ref.shape)
    last = ids_row[:, count - 1 :]
    start = jnp.int32(0)
    latest = jnp.int32(0)
    for d in range(lengths_ref.shape[0]):
        latest = jnp.where(start < first, start, latest)
        start = start + lengths_ref[d]
    back = jnp.int32(0)
    for i in range(1, most):
        back = back + jnp.where(latest < first - i * count, 1, 0)
    flags_ref[0:1, :] = (ids_row == last).astype(F32)
    flags_ref[1:2, :] = jnp.broadcast_to((last == before).astype(F32), (1, count))
    flags_ref[2:3, :] = jnp.full((1, count), back.astype(F32))


def span_heads(head, k_ref, v_ref, beta_ref, g_ref, strict_ref, flags_ref, refs):
    count = k_ref.shape[0]
    up_ref, half_ref, kneg_refs, update_refs = refs[0], refs[1], refs[2:4], refs[4:6]
    width = refs[6].shape[1]
    places = [(a, b, i) for a, b in zip(refs[6::2], refs[7::2]) for i in range(a.shape[0])]
    heads = range(len(places))
    here = [slice((head + h) * width, (head + h + 1) * width) for h in heads]
    own = [slice(h * width, (h + 1) * width) for h in heads]
    row = lax.broadcasted_iota(jnp.int32, (count, count), 0)
    sums = (row >= lanes_of((count, count))).astype(F32).astype(BF16)
    cumul_all = dot(sums, g_ref[:, here[0].start : here[-1].stop])
    eye = lax.broadcasted_iota(jnp.int32, (width, width), 0) == lanes_of((width, width))
    strength = [beta_ref[head + h : head + h + 1, :] for h in heads]
    tail = flags_ref[0:1, :]
    kept = flags_ref[1:2, :width]
    total, kneg, kpos, khat, parts = [], [], [], [], []
    for h in heads:
        cumul = cumul_all[:, own[h]]
        total.append(cumul[count - 1 :, :])
        middle = total[h] * 0.5
        half = jnp.exp(middle)
        up = jnp.exp(cumul - middle)
        up_ref[:, own[h]] = up
        half_ref[0:1, own[h]] = half
        kn = unit_rows(k_ref[:, here[h]].astype(F32))
        negative = kn * jnp.exp(middle - cumul)
        kneg.append(halves(negative))
        for ref, x in zip(kneg_refs, kneg[h]):
            ref[:, own[h]] = x
        kpos.append(kn * up)
        parts.append(halves(kpos[h] * half))
        khat.append(halves((negative * half).T * (strength[h] * tail)))
    strict = strict_ref[...] > 0.0
    systems = [
        jnp.where(strict, dot3(halves(kpos[h]), kneg[h], ((1,), (1,))) * strength[h], 0.0)
        for h in heads
    ]
    rights = []
    for h in heads:
        value = v_ref[:, here[h]]
        rights.append(
            (
                jnp.concatenate([value, parts[h][0]], axis=1),
                jnp.concatenate([jnp.zeros_like(value), parts[h][1]], axis=1),
            )
        )
    updates = solve(systems, rights, count)
    for h in heads:
        for ref, x in zip(update_refs, updates[h]):
            ref[:, 2 * h * width : 2 * (h + 1) * width] = x
        found = dot3(khat[h], updates[h])
        a_ref, b_ref, i = places[h]
        b_ref[i] = found[:, :width]
        a_ref[i] = (jnp.where(eye, jnp.exp(total[h]), 0.0) - found[:, width:]) * kept


def query_kernel(head, q_ref, beta_ref, lower_ref, fresh_ref, flags_ref, *refs):
    up_ref, half_ref, kneg_refs, update_refs = refs[0], refs[1], refs[2:4], refs[4:6]
    out_ref, reach_ref = refs[6:]
    count, width = fresh_ref.shape
    heads = range(out_ref.shape[1] // width)
    own = [slice(h * width, (h + 1) * width) for h in heads]
    lower = lower_ref[...] > 0.0
    fresh = fresh_ref[...] > 0.0
    qpos = [
        unit_rows(q_ref[:, (head + h) * width : (head + h + 1) * width].astype(F32))
        * up_ref[:, own[h]]
        for h in heads
    ]
    scores = []
    for h in heads:
        kneg = tuple(x[:, own[h]] for x in kneg_refs)
        product = dot3(halves(qpos[h]), kneg, ((1,), (1,)))
        scores.append(
            halves(jnp.where(lower, product * beta_ref[head + h : head + h + 1, :], 0.0))
        )
    for h in heads:
        update = tuple(x[:, 2 * h * width : 2 * (h + 1) * width] for x in update_refs)
        found = dot3(scores[h], update)
        out_ref[:, own[h]] = found[:, :width]
        reach_ref[:, own[h]] = jnp.where(
            fresh, qpos[h] * half_ref[0:1, own[h]] - found[:, width:], 0.0
        )


def query(head, shared, flags, saved):
    beta, queries, _, _, _, _, lower, fresh = shared
    count = queries.shape[0]
    part = jax.ShapeDtypeStruct(saved[0].shape, F32)
    given = [queries, beta, lower, fresh, flags, *saved]
    return pl.pallas_call(
        functools.partial(query_kernel, head),
        in_specs=[VMEM] * len(given),
        out_specs=[VMEM] * 2,
        out_shape=[part, part],
        compiler_params=pltpu.CompilerParams(vmem_limit_bytes=32 << 20),
        cost_estimate=QUERY,
        name="query",
    )(*given)


VMEM = pl.BlockSpec(memory_space=pltpu.VMEM)
ANY = pl.BlockSpec(memory_space=pl.ANY)


def opening_kernel(most, *refs):
    lengths_hbm, beta_hbm, *sources = refs[:6]
    beta_ref, *targets = refs[6:11]
    masks = refs[11:15]
    outs = refs[15:-2]
    lengths_ref, sems = refs[-2:]
    count = sources[0].shape[0]
    cols = outs[0].shape[1]
    first = [(lengths_hbm, lengths_ref), (beta_hbm, beta_ref)]
    pairs = list(zip(sources, targets))
    first += [(x.at[:, :cols], y.at[:, :cols]) for x, y in pairs[1:]]
    rest = [(x.at[:, cols:], y.at[:, cols:]) for x, y in pairs[1:]] + pairs[:1]
    copies = [pltpu.make_async_copy(x, y, sems.at[i]) for i, (x, y) in enumerate(first + rest)]
    for copy in copies:
        copy.start()
    copies[0].wait()
    documents(lengths_ref, count, most, *masks)
    for copy in copies[1 : len(first)]:
        copy.wait()
    _, k_ref, v_ref, g_ref = targets
    strict_ref, _, _, flags_ref = masks
    span_heads(0, k_ref, v_ref, beta_ref, g_ref, strict_ref, flags_ref, outs)
    for copy in copies[len(first) :]:
        copy.wait()


def span_shapes(groups, count, width):
    cols = sum(groups) * width
    shapes = [((count, cols), F32), ((8, cols), F32)]
    shapes += [((count, cols), BF16)] * 2 + [((count, 2 * cols), BF16)] * 2
    shapes += [((x, width, width), F32) for x in groups for _ in range(2)]
    return [jax.ShapeDtypeStruct(*x) for x in shapes]


def opening(groups, most, lengths, strength, queries, keys, values, log_decay):
    count, total = queries.shape
    heads = strength.shape[0]
    width = total // heads
    given = [lengths, strength, queries, keys, values, log_decay]
    given = [pltpu.with_memory_space_constraint(x, pltpu.HBM) for x in given]
    square = jax.ShapeDtypeStruct((count, count), F32)
    kept = [jax.ShapeDtypeStruct(x.shape, x.dtype) for x in given[1:]]
    kept += [
        square,
        square,
        jax.ShapeDtypeStruct((count, width), F32),
        jax.ShapeDtypeStruct((8, count), F32),
    ]
    shapes = kept + span_shapes(groups, count, width)
    results = pl.pallas_call(
        functools.partial(opening_kernel, most),
        in_specs=[ANY] * len(given),
        out_specs=[VMEM] * len(shapes),
        out_shape=shapes,
        scratch_shapes=[pltpu.SMEM(lengths.shape, lengths.dtype), pltpu.SemaphoreType.DMA((9,))],
        compiler_params=pltpu.CompilerParams(vmem_limit_bytes=32 << 20),
        cost_estimate=COST,
        name="opening",
    )(*given)
    return results[: len(kept)], results[len(kept) :]


def span_kernel(head, k_ref, v_ref, beta_ref, g_ref, strict_ref, flags_ref, *refs):
    span_heads(head, k_ref, v_ref, beta_ref, g_ref, strict_ref, flags_ref, refs)


def span(head, groups, shared, flags):
    beta, queries, keys, values, decay, strict, _, _ = shared
    count = keys.shape[0]
    given = [keys, values, beta, decay, strict, flags]
    shapes = span_shapes(groups, count, keys.shape[1] // beta.shape[0])
    return pl.pallas_call(
        functools.partial(span_kernel, head),
        in_specs=[VMEM] * len(given),
        out_specs=[VMEM] * len(shapes),
        out_shape=shapes,
        compiler_params=pltpu.CompilerParams(vmem_limit_bytes=32 << 20),
        cost_estimate=COST,
        name="span",
    )(*given)


def pass_kernel(own, low, late, flags_ref, state_ref, *refs):
    out_ref = refs[-1]
    width = out_ref.shape[1]
    before = flags_ref[2:3, :width]
    kept = flags_ref[1:2, :width] > 0.0
    for h in range(out_ref.shape[0]):
        there = [i for i in range(late) if h < refs[own + 2 * i].shape[0]]
        sent = None
        if there:
            trans_a, trans_b = refs[own + 2 * there[0]][h], refs[own + 2 * there[0] + 1][h]
            for i in there[1:]:
                here = before == low + i
                trans_a = jnp.where(here, refs[own + 2 * i][h], trans_a)
                trans_b = jnp.where(here, refs[own + 2 * i + 1][h], trans_b)
            sent = trans_b + dot3(halves(trans_a), halves(state_ref[h]))
        if own and h < refs[0].shape[0]:
            sent = refs[0][h] if sent is None else jnp.where(kept, sent, refs[0][h])
        out_ref[h] = sent


def message(step, most, flags, trans_a, trans_b, received):
    own = [trans_b[step]] if step < len(trans_b) else []
    if step < LAG:
        return own[0]
    late = [step - LAG * i for i in range(1, most)]
    low = next(i for i, x in enumerate(late) if x < len(trans_b))
    late = [x for x in late if 0 <= x < len(trans_b)]
    carried = [x for g in late for x in (trans_a[g], trans_b[g])]
    size = max(x.shape[0] for x in own + carried)
    return pl.pallas_call(
        functools.partial(pass_kernel, len(own), low, len(late)),
        in_specs=[VMEM] * (2 + len(own) + len(carried)),
        out_specs=VMEM,
        out_shape=jax.ShapeDtypeStruct((size, *trans_b[0].shape[1:]), F32),
        compiler_params=pltpu.CompilerParams(vmem_limit_bytes=8 << 20),
        cost_estimate=PASS,
        name="pass_on",
    )(flags, received[step - LAG], *own, *carried)


def finish_kernel(parts, most, flags_ref, gain_ref, *refs):
    mixed_hbm, buffer, sems = refs[-3:]
    width = refs[2].shape[1]
    before = flags_ref[2:3, :width]
    copies, filled = [], 0
    for n, (head, at, size) in enumerate(parts):
        outs_ref, reach_ref, *states = refs[n * (most + 2) : (n + 1) * (most + 2)]
        for h in range(size):
            here = slice((at + h) * width, (at + h + 1) * width)
            state = states[0][h]
            for i in range(1, most):
                state = jnp.where(before == i, states[i][h], state)
            total = outs_ref[:, here] + dot3(halves(reach_ref[:, here]), halves(state))
            scale = lax.rsqrt(jnp.mean(total * total, axis=-1, keepdims=True) + 1e-06)
            there = slice((head + h) * width, (head + h + 1) * width)
            place = slice((filled + h) * width, (filled + h + 1) * width)
            buffer[:, place] = (total * scale * gain_ref[:, there]).astype(BF16)
        there = slice(head * width, (head + size) * width)
        place = slice(filled * width, (filled + size) * width)
        copies.append(
            pltpu.make_async_copy(buffer.at[:, place], mixed_hbm.at[:, there], sems.at[n])
        )
        copies[-1].start()
        filled += size
    for copy in copies:
        copy.wait()


def finished(chosen, places, mixed, flags, answers, received, most, gain):
    count = answers[0][0].shape[0]
    width = received[0].shape[1]
    given = [flags, gain]
    for g in chosen:
        given += [*answers[g], *(received[g + LAG * i] for i in range(most))]
    specs = [VMEM] * len(given)
    aliases = {}
    parts = [places[g] for g in chosen]
    kernel = functools.partial(finish_kernel, parts, most)
    if mixed is not None:
        aliases = {len(given): 0}
        given.append(mixed)
        specs.append(ANY)
        kernel = functools.partial(finish_more, parts, most)
    return pl.pallas_call(
        kernel,
        in_specs=specs,
        out_specs=pl.BlockSpec(memory_space=pltpu.HBM),
        out_shape=jax.ShapeDtypeStruct((count, gain.shape[1]), BF16),
        scratch_shapes=[
            pltpu.VMEM((count, sum(x[2] for x in parts) * width), BF16),
            pltpu.SemaphoreType.DMA((len(parts),)),
        ],
        input_output_aliases=aliases,
        compiler_params=pltpu.CompilerParams(vmem_limit_bytes=16 << 20),
        cost_estimate=END,
        name="finish",
    )(*given)


def finish_more(parts, most, *refs):
    finish_kernel(parts, most, *refs[:-4], *refs[-3:])


def then(flags, results):
    flags, results = lax.optimization_barrier((flags, tuple(results)))
    return flags, list(results)


def local(queries, keys, values, beta, log_decay, out_gain, doc_lengths):
    devices = lax.axis_size("ctx")
    ring = [(i, (i + 1) % devices) for i in range(devices)]
    most = devices // 2
    gain = out_gain.reshape(1, -1)
    sizes = [x for s in SPANS for x in s]
    groups = len(sizes)
    places, spans, head = [], [], 0
    for n, span_groups in enumerate(SPANS):
        for i, size in enumerate(span_groups):
            places.append((head + sum(span_groups[:i]), sum(span_groups[:i]), size))
            spans.append(n)
        head += sum(span_groups)
    shared, first = opening(SPANS[0], most, doc_lengths, beta.T, queries, keys, values, log_decay)
    shared, flags = shared[:-1], shared[-1]
    flags, first = then(flags, first)
    found = [first]
    trans_a, trans_b = first[6::2], first[7::2]
    received = []
    mixed = None
    answers = []
    starts = [sum(map(sum, SPANS[:n])) for n in range(len(SPANS))]
    for step in range(groups + LAG * (most - 1)):
        if step < groups and spans[step] == len(found):
            flags, results = then(flags, span(places[step][0], SPANS[spans[step]], shared, flags))
            found.append(results)
            trans_a, trans_b = trans_a + results[6::2], trans_b + results[7::2]
        sent = message(step, most, flags, trans_a, trans_b, received)
        if step >= LAG:
            flags, (sent,) = then(flags, [sent])
        received.append(lax.ppermute(sent, "ctx", ring))
        for _ in range(FILL[max(0, step - groups + 1)] if step >= groups - 1 else 0):
            if len(answers) < len(found):
                n = len(answers)
                flags, results = then(flags, query(starts[n], shared, flags, found[n][:6]))
                answers.append(results)
    for n in range(len(answers), len(found)):
        flags, results = then(flags, query(starts[n], shared, flags, found[n][:6]))
        answers.append(results)
    answers = [answers[n] for n in spans]
    for chosen in (range(groups - LATE), *([g] for g in range(groups - LATE, groups))):
        mixed = finished(chosen, places, mixed, flags, answers, received, most, gain)
    return mixed


def solution(mesh):
    rows = P(("dp", "ctx"), None)
    return jax.shard_map(
        local,
        mesh=mesh,
        in_specs=(rows, rows, rows, rows, rows, P(), P("dp")),
        out_specs=rows,
        check_vma=False,
    )
```

```python
import functools

import jax
import jax.numpy as jnp
from jax import lax
from jax.experimental import pallas as pl
from jax.experimental.pallas import tpu as pltpu
from jax.sharding import PartitionSpec as P

F32 = jnp.float32
BF16 = jnp.bfloat16
TILE = 16
BLOCK = 64
SPANS = ((2,), (2, 2), (2, 2), (2, 2), (2,))
LAG = 3
FILL = (1,) * 99
LATE = 2
QUERY = pl.CostEstimate(flops=10**8, transcendentals=0, bytes_accessed=1)
COST = pl.CostEstimate(flops=10**8, transcendentals=0, bytes_accessed=1)
PASS = pl.CostEstimate(flops=10**6, transcendentals=0, bytes_accessed=1)
END = pl.CostEstimate(flops=10**8, transcendentals=0, bytes_accessed=1)


def halves(x):
    high = x.astype(BF16)
    return high, (x - high.astype(F32)).astype(BF16)


def dot(a, b, dims=((1,), (0,))):
    return lax.dot_general(a, b, (dims, ((), ())), preferred_element_type=F32)


def dot3(a, b, dims=((1,), (0,))):
    rows = a[0].shape[0]
    both = dot(jnp.concatenate(a, axis=0), b[0], dims)
    return both[:rows] + (dot(a[0], b[1], dims) + both[rows:])


def rows_of(pair, low, high):
    return pair[0][low:high], pair[1][low:high]


def unit_rows(x):
    return x * lax.rsqrt(jnp.sum(x * x, axis=-1, keepdims=True) + 1e-06)


def doc_ids(lengths_ref, first, shape, dim):
    place = first + lax.broadcasted_iota(jnp.int32, shape, dim)
    ids = jnp.zeros(shape, jnp.int32)
    before = jnp.int32(0)
    start = jnp.int32(0)
    for d in range(lengths_ref.shape[0]):
        ids = ids + (place >= start).astype(jnp.int32)
        before = before + (first > start).astype(jnp.int32)
        start = start + lengths_ref[d]
    return ids, before


def lanes_of(shape):
    return lax.broadcasted_iota(jnp.int32, shape, 1)


def side_by_side(system, count, size):
    lane = lanes_of((size, count)) // size
    side = system[:size]
    for b in range(1, count // size):
        side = jnp.where(lane == b, system[b * size : (b + 1) * size], side)
    return side


def tile_inverses(systems, count):
    sides = [side_by_side(s, count, TILE) for s in systems]
    whole = count // 128 * 128
    pieces = [s[:, low : low + 128] for s in sides for low in range(0, whole, 128)]
    rest = [s[:, whole:] for s in sides]
    if count > whole:
        for i in range(0, len(rest), 128 // (count - whole)):
            group = rest[i : i + 128 // (count - whole)]
            wide = sum(x.shape[1] for x in group)
            if wide < 128:
                group = group + [jnp.zeros((TILE, 128 - wide), F32)]
            pieces.append(jnp.concatenate(group, axis=1))
    lane = lanes_of((TILE, 128))
    home = lane - lane % TILE
    eye = (lane % TILE == lax.broadcasted_iota(jnp.int32, (TILE, 128), 0)).astype(F32)
    found = [[eye[8 * i : 8 * i + 8] for i in range(TILE // 8)] for _ in pieces]
    for j in range(TILE - 1):
        for p, piece in enumerate(pieces):
            line = found[p][j // 8][j % 8 : j % 8 + 1, :]
            for i in range((j + 1) // 8, TILE // 8):
                column = jnp.take_along_axis(
                    piece[8 * i : 8 * i + 8], home[:8] + j, axis=1, mode="promise_in_bounds"
                )
                found[p][i] = found[p][i] - column * line
    found = [jnp.concatenate(x, axis=0) for x in found]
    each = whole // 128
    results = []
    for h in range(len(systems)):
        parts = found[h * each : (h + 1) * each]
        if count > whole:
            per = 128 // (count - whole)
            at = h % per * (count - whole)
            parts = parts + [found[each * len(systems) + h // per][:, at : at + count - whole]]
        results.append(jnp.concatenate(parts, axis=1))
    return results


def spread(side, count, height, column_of):
    block = column_of(lanes_of(side.shape) // height)
    return jnp.concatenate([jnp.where(block == b, side, 0.0) for b in range(count // height)], axis=0)


def merged(system, side, count, size):
    lane = lanes_of(side.shape) // size
    even = lane % 2 == 0
    below = jnp.zeros(side.shape, F32)
    for b in range(1, count // size, 2):
        below = jnp.where(lane == b - 1, system[b * size : (b + 1) * size, :], below)
    wide = spread(side, count, size, lambda x: x)
    middle = dot3(halves(below), halves(wide))
    tall = spread(middle, count, size, lambda x: jnp.where(x % 2 == 0, x + 1, -1))
    corner = dot3(halves(jnp.where(even, 0.0, side)), halves(tall))
    return jnp.concatenate([jnp.where(even, side, 0.0), jnp.where(even, -corner, side)], axis=0)


def solve(systems, rights, count):
    sides = tile_inverses(systems, count)
    size = TILE
    while size < BLOCK:
        sides = [merged(s, x, count, size) for s, x in zip(systems, sides)]
        size = 2 * size
    wides = [halves(spread(x, count, BLOCK, lambda x: x)) for x in sides]
    row = lax.broadcasted_iota(jnp.int32, (count, count), 0) // BLOCK
    outside = row > lanes_of((count, count)) // BLOCK
    splits = [halves(jnp.where(outside, s, 0.0)) for s in systems]
    firsts = [dot3(w, r) for w, r in zip(wides, rights)]
    links = [halves(dot3(rows_of(w, BLOCK, count), s)) for w, s in zip(wides, splits)]
    done = [halves(x[:BLOCK]) for x in firsts]
    for b in range(1, count // BLOCK):
        low, high = b * BLOCK, (b + 1) * BLOCK
        for h in range(len(systems)):
            link = tuple(x[low - BLOCK : low, :low] for x in links[h])
            part = halves(firsts[h][low:high] - dot3(link, done[h]))
            done[h] = tuple(jnp.concatenate(x, axis=0) for x in zip(done[h], part))
    return done


def documents(lengths_ref, count, most, strict_ref, lower_ref, fresh_ref, flags_ref):
    first = lax.axis_index("ctx") * count
    ids_col, before = doc_ids(lengths_ref, first, (count, 1), 0)
    ids_row, _ = doc_ids(lengths_ref, first, (1, count), 1)
    row = lax.broadcasted_iota(jnp.int32, (count, count), 0)
    col = lanes_of((count, count))
    same = ids_col == ids_row
    lower_ref[...] = (same & (row >= col)).astype(F32)
    strict_ref[...] = (same & (row > col)).astype(F32)
    fresh_ref[...] = jnp.broadcast_to((ids_col == before).astype(F32), fresh_ref.shape)
    last = ids_row[:, count - 1 :]
    start = jnp.int32(0)
    latest = jnp.int32(0)
    for d in range(lengths_ref.shape[0]):
        latest = jnp.where(start < first, start, latest)
        start = start + lengths_ref[d]
    back = jnp.int32(0)
    for i in range(1, most):
        back = back + jnp.where(latest < first - i * count, 1, 0)
    flags_ref[0:1, :] = (ids_row == last).astype(F32)
    flags_ref[1:2, :] = jnp.broadcast_to((last == before).astype(F32), (1, count))
    flags_ref[2:3, :] = jnp.full((1, count), back.astype(F32))


def span_heads(head, k_ref, v_ref, beta_ref, g_ref, strict_ref, flags_ref, refs):
    count = k_ref.shape[0]
    up_ref, half_ref, kneg_refs, update_refs = refs[0], refs[1], refs[2:4], refs[4:6]
    width = refs[6].shape[1]
    places = [(a, b, i) for a, b in zip(refs[6::2], refs[7::2]) for i in range(a.shape[0])]
    heads = range(len(places))
    here = [slice((head + h) * width, (head + h + 1) * width) for h in heads]
    own = [slice(h * width, (h + 1) * width) for h in heads]
    row = lax.broadcasted_iota(jnp.int32, (count, count), 0)
    sums = (row >= lanes_of((count, count))).astype(F32).astype(BF16)
    cumul_all = dot(sums, g_ref[:, here[0].start : here[-1].stop])
    eye = lax.broadcasted_iota(jnp.int32, (width, width), 0) == lanes_of((width, width))
    strength = [beta_ref[head + h : head + h + 1, :] for h in heads]
    tail = flags_ref[0:1, :]
    kept = flags_ref[1:2, :width]
    total, kneg, kpos, khat, parts = [], [], [], [], []
    for h in heads:
        cumul = cumul_all[:, own[h]]
        total.append(cumul[count - 1 :, :])
        middle = total[h] * 0.5
        half = jnp.exp(middle)
        up = jnp.exp(cumul - middle)
        up_ref[:, own[h]] = up
        half_ref[0:1, own[h]] = half
        kn = unit_rows(k_ref[:, here[h]].astype(F32))
        negative = kn * jnp.exp(middle - cumul)
        kneg.append(halves(negative))
        for ref, x in zip(kneg_refs, kneg[h]):
            ref[:, own[h]] = x
        kpos.append(kn * up)
        parts.append(halves(kpos[h] * half))
        khat.append(halves((negative * half).T * (strength[h] * tail)))
    strict = strict_ref[...] > 0.0
    systems = [
        jnp.where(strict, dot3(halves(kpos[h]), kneg[h], ((1,), (1,))) * strength[h], 0.0)
        for h in heads
    ]
    rights = []
    for h in heads:
        value = v_ref[:, here[h]]
        rights.append(
            (
                jnp.concatenate([value, parts[h][0]], axis=1),
                jnp.concatenate([jnp.zeros_like(value), parts[h][1]], axis=1),
            )
        )
    updates = solve(systems, rights, count)
    for h in heads:
        for ref, x in zip(update_refs, updates[h]):
            ref[:, 2 * h * width : 2 * (h + 1) * width] = x
        found = dot3(khat[h], updates[h])
        a_ref, b_ref, i = places[h]
        b_ref[i] = found[:, :width]
        a_ref[i] = (jnp.where(eye, jnp.exp(total[h]), 0.0) - found[:, width:]) * kept


def query_kernel(head, q_ref, beta_ref, lower_ref, fresh_ref, flags_ref, *refs):
    up_ref, half_ref, kneg_refs, update_refs = refs[0], refs[1], refs[2:4], refs[4:6]
    out_ref, reach_ref = refs[6:]
    count, width = fresh_ref.shape
    heads = range(out_ref.shape[1] // width)
    own = [slice(h * width, (h + 1) * width) for h in heads]
    lower = lower_ref[...] > 0.0
    fresh = fresh_ref[...] > 0.0
    qpos = [
        unit_rows(q_ref[:, (head + h) * width : (head + h + 1) * width].astype(F32))
        * up_ref[:, own[h]]
        for h in heads
    ]
    scores = []
    for h in heads:
        kneg = tuple(x[:, own[h]] for x in kneg_refs)
        product = dot3(halves(qpos[h]), kneg, ((1,), (1,)))
        scores.append(
            halves(jnp.where(lower, product * beta_ref[head + h : head + h + 1, :], 0.0))
        )
    for h in heads:
        update = tuple(x[:, 2 * h * width : 2 * (h + 1) * width] for x in update_refs)
        found = dot3(scores[h], update)
        out_ref[:, own[h]] = found[:, :width]
        reach_ref[:, own[h]] = jnp.where(
            fresh, qpos[h] * half_ref[0:1, own[h]] - found[:, width:], 0.0
        )


def query(head, shared, flags, saved):
    beta, queries, _, _, _, _, lower, fresh = shared
    count = queries.shape[0]
    part = jax.ShapeDtypeStruct(saved[0].shape, F32)
    given = [queries, beta, lower, fresh, flags, *saved]
    return pl.pallas_call(
        functools.partial(query_kernel, head),
        in_specs=[VMEM] * len(given),
        out_specs=[VMEM] * 2,
        out_shape=[part, part],
        compiler_params=pltpu.CompilerParams(vmem_limit_bytes=32 << 20),
        cost_estimate=QUERY,
        name="query",
    )(*given)


VMEM = pl.BlockSpec(memory_space=pltpu.VMEM)
ANY = pl.BlockSpec(memory_space=pl.ANY)


def opening_kernel(most, *refs):
    lengths_hbm, beta_hbm, *sources = refs[:6]
    beta_ref, *targets = refs[6:11]
    masks = refs[11:15]
    outs = refs[15:-2]
    lengths_ref, sems = refs[-2:]
    count = sources[0].shape[0]
    cols = outs[0].shape[1]
    first = [(lengths_hbm, lengths_ref), (beta_hbm, beta_ref)]
    pairs = list(zip(sources, targets))
    first += [(x.at[:, :cols], y.at[:, :cols]) for x, y in pairs[1:]]
    rest = [(x.at[:, cols:], y.at[:, cols:]) for x, y in pairs[1:]] + pairs[:1]
    copies = [pltpu.make_async_copy(x, y, sems.at[i]) for i, (x, y) in enumerate(first + rest)]
    for copy in copies:
        copy.start()
    copies[0].wait()
    documents(lengths_ref, count, most, *masks)
    for copy in copies[1 : len(first)]:
        copy.wait()
    _, k_ref, v_ref, g_ref = targets
    strict_ref, _, _, flags_ref = masks
    span_heads(0, k_ref, v_ref, beta_ref, g_ref, strict_ref, flags_ref, outs)
    for copy in copies[len(first) :]:
        copy.wait()


def span_shapes(groups, count, width):
    cols = sum(groups) * width
    shapes = [((count, cols), F32), ((8, cols), F32)]
    shapes += [((count, cols), BF16)] * 2 + [((count, 2 * cols), BF16)] * 2
    shapes += [((x, width, width), F32) for x in groups for _ in range(2)]
    return [jax.ShapeDtypeStruct(*x) for x in shapes]


def opening(groups, most, lengths, strength, queries, keys, values, log_decay):
    count, total = queries.shape
    heads = strength.shape[0]
    width = total // heads
    given = [lengths, strength, queries, keys, values, log_decay]
    given = [pltpu.with_memory_space_constraint(x, pltpu.HBM) for x in given]
    square = jax.ShapeDtypeStruct((count, count), F32)
    kept = [jax.ShapeDtypeStruct(x.shape, x.dtype) for x in given[1:]]
    kept += [
        square,
        square,
        jax.ShapeDtypeStruct((count, width), F32),
        jax.ShapeDtypeStruct((8, count), F32),
    ]
    shapes = kept + span_shapes(groups, count, width)
    results = pl.pallas_call(
        functools.partial(opening_kernel, most),
        in_specs=[ANY] * len(given),
        out_specs=[VMEM] * len(shapes),
        out_shape=shapes,
        scratch_shapes=[pltpu.SMEM(lengths.shape, lengths.dtype), pltpu.SemaphoreType.DMA((9,))],
        compiler_params=pltpu.CompilerParams(vmem_limit_bytes=32 << 20),
        cost_estimate=COST,
        name="opening",
    )(*given)
    return results[: len(kept)], results[len(kept) :]


def span_kernel(head, k_ref, v_ref, beta_ref, g_ref, strict_ref, flags_ref, *refs):
    span_heads(head, k_ref, v_ref, beta_ref, g_ref, strict_ref, flags_ref, refs)


def span(head, groups, shared, flags):
    beta, queries, keys, values, decay, strict, _, _ = shared
    count = keys.shape[0]
    given = [keys, values, beta, decay, strict, flags]
    shapes = span_shapes(groups, count, keys.shape[1] // beta.shape[0])
    return pl.pallas_call(
        functools.partial(span_kernel, head),
        in_specs=[VMEM] * len(given),
        out_specs=[VMEM] * len(shapes),
        out_shape=shapes,
        compiler_params=pltpu.CompilerParams(vmem_limit_bytes=32 << 20),
        cost_estimate=COST,
        name="span",
    )(*given)


def pass_kernel(own, low, late, flags_ref, state_ref, *refs):
    out_ref = refs[-1]
    width = out_ref.shape[1]
    before = flags_ref[2:3, :width]
    kept = flags_ref[1:2, :width] > 0.0
    for h in range(out_ref.shape[0]):
        there = [i for i in range(late) if h < refs[own + 2 * i].shape[0]]
        sent = None
        if there:
            trans_a, trans_b = refs[own + 2 * there[0]][h], refs[own + 2 * there[0] + 1][h]
            for i in there[1:]:
                here = before == low + i
                trans_a = jnp.where(here, refs[own + 2 * i][h], trans_a)
                trans_b = jnp.where(here, refs[own + 2 * i + 1][h], trans_b)
            sent = trans_b + dot3(halves(trans_a), halves(state_ref[h]))
        if own and h < refs[0].shape[0]:
            sent = refs[0][h] if sent is None else jnp.where(kept, sent, refs[0][h])
        out_ref[h] = sent


def message(step, most, flags, trans_a, trans_b, received):
    own = [trans_b[step]] if step < len(trans_b) else []
    if step < LAG:
        return own[0]
    late = [step - LAG * i for i in range(1, most)]
    low = next(i for i, x in enumerate(late) if x < len(trans_b))
    late = [x for x in late if 0 <= x < len(trans_b)]
    carried = [x for g in late for x in (trans_a[g], trans_b[g])]
    size = max(x.shape[0] for x in own + carried)
    return pl.pallas_call(
        functools.partial(pass_kernel, len(own), low, len(late)),
        in_specs=[VMEM] * (2 + len(own) + len(carried)),
        out_specs=VMEM,
        out_shape=jax.ShapeDtypeStruct((size, *trans_b[0].shape[1:]), F32),
        compiler_params=pltpu.CompilerParams(vmem_limit_bytes=8 << 20),
        cost_estimate=PASS,
        name="pass_on",
    )(flags, received[step - LAG], *own, *carried)


def finish_kernel(parts, most, flags_ref, gain_ref, *refs):
    mixed_hbm, buffer, sems = refs[-3:]
    width = refs[2].shape[1]
    before = flags_ref[2:3, :width]
    copies, filled = [], 0
    for n, (head, at, size) in enumerate(parts):
        outs_ref, reach_ref, *states = refs[n * (most + 2) : (n + 1) * (most + 2)]
        for h in range(size):
            here = slice((at + h) * width, (at + h + 1) * width)
            state = states[0][h]
            for i in range(1, most):
                state = jnp.where(before == i, states[i][h], state)
            total = outs_ref[:, here] + dot3(halves(reach_ref[:, here]), halves(state))
            scale = lax.rsqrt(jnp.mean(total * total, axis=-1, keepdims=True) + 1e-06)
            there = slice((head + h) * width, (head + h + 1) * width)
            place = slice((filled + h) * width, (filled + h + 1) * width)
            buffer[:, place] = (total * scale * gain_ref[:, there]).astype(BF16)
        there = slice(head * width, (head + size) * width)
        place = slice(filled * width, (filled + size) * width)
        copies.append(
            pltpu.make_async_copy(buffer.at[:, place], mixed_hbm.at[:, there], sems.at[n])
        )
        copies[-1].start()
        filled += size
    for copy in copies:
        copy.wait()


def finished(chosen, places, mixed, flags, answers, received, most, gain):
    count = answers[0][0].shape[0]
    width = received[0].shape[1]
    given = [flags, gain]
    for g in chosen:
        given += [*answers[g], *(received[g + LAG * i] for i in range(most))]
    specs = [VMEM] * len(given)
    aliases = {}
    parts = [places[g] for g in chosen]
    kernel = functools.partial(finish_kernel, parts, most)
    if mixed is not None:
        aliases = {len(given): 0}
        given.append(mixed)
        specs.append(ANY)
        kernel = functools.partial(finish_more, parts, most)
    return pl.pallas_call(
        kernel,
        in_specs=specs,
        out_specs=pl.BlockSpec(memory_space=pltpu.HBM),
        out_shape=jax.ShapeDtypeStruct((count, gain.shape[1]), BF16),
        scratch_shapes=[
            pltpu.VMEM((count, sum(x[2] for x in parts) * width), BF16),
            pltpu.SemaphoreType.DMA((len(parts),)),
        ],
        input_output_aliases=aliases,
        compiler_params=pltpu.CompilerParams(vmem_limit_bytes=16 << 20),
        cost_estimate=END,
        name="finish",
    )(*given)


def finish_more(parts, most, *refs):
    finish_kernel(parts, most, *refs[:-4], *refs[-3:])


def then(flags, results):
    flags, results = lax.optimization_barrier((flags, tuple(results)))
    return flags, list(results)


def local(queries, keys, values, beta, log_decay, out_gain, doc_lengths):
    devices = lax.axis_size("ctx")
    ring = [(i, (i + 1) % devices) for i in range(devices)]
    most = devices // 2
    gain = out_gain.reshape(1, -1)
    sizes = [x for s in SPANS for x in s]
    groups = len(sizes)
    places, spans, head = [], [], 0
    for n, span_groups in enumerate(SPANS):
        for i, size in enumerate(span_groups):
            places.append((head + sum(span_groups[:i]), sum(span_groups[:i]), size))
            spans.append(n)
        head += sum(span_groups)
    shared, first = opening(SPANS[0], most, doc_lengths, beta.T, queries, keys, values, log_decay)
    shared, flags = shared[:-1], shared[-1]
    flags, first = then(flags, first)
    found = [first]
    trans_a, trans_b = first[6::2], first[7::2]
    received = []
    mixed = None
    answers = []
    starts = [sum(map(sum, SPANS[:n])) for n in range(len(SPANS))]
    for step in range(groups + LAG * (most - 1)):
        if step < groups and spans[step] == len(found):
            flags, results = then(flags, span(places[step][0], SPANS[spans[step]], shared, flags))
            found.append(results)
            trans_a, trans_b = trans_a + results[6::2], trans_b + results[7::2]
        sent = message(step, most, flags, trans_a, trans_b, received)
        if step >= LAG:
            flags, (sent,) = then(flags, [sent])
        received.append(lax.ppermute(sent, "ctx", ring))
        for _ in range(FILL[max(0, step - groups + 1)] if step >= groups - 1 else 0):
            if len(answers) < len(found):
                n = len(answers)
                flags, results = then(flags, query(starts[n], shared, flags, found[n][:6]))
                answers.append(results)
    for n in range(len(answers), len(found)):
        flags, results = then(flags, query(starts[n], shared, flags, found[n][:6]))
        answers.append(results)
    answers = [answers[n] for n in spans]
    for chosen in (range(groups - LATE), *([g] for g in range(groups - LATE, groups))):
        mixed = finished(chosen, places, mixed, flags, answers, received, most, gain)
    return mixed


def solution(mesh):
    rows = P(("dp", "ctx"), None)
    return jax.shard_map(
        local,
        mesh=mesh,
        in_specs=(rows, rows, rows, rows, rows, P(), P("dp")),
        out_specs=rows,
        check_vma=False,
    )
```

```python
import functools

import jax
import jax.numpy as jnp
from jax import lax
from jax.experimental import pallas as pl
from jax.experimental.pallas import tpu as pltpu
from jax.sharding import PartitionSpec as P

F32 = jnp.float32
BF16 = jnp.bfloat16
TILE = 16
BLOCK = 64
SPANS = ((2,), (2, 2, 2), (2, 2, 2, 2))
LAG = 3
FILL = (1,) * 99
LATE = 2
QUERY = pl.CostEstimate(flops=10**8, transcendentals=0, bytes_accessed=1)
COST = pl.CostEstimate(flops=10**8, transcendentals=0, bytes_accessed=1)
PASS = pl.CostEstimate(flops=10**6, transcendentals=0, bytes_accessed=1)
END = pl.CostEstimate(flops=10**8, transcendentals=0, bytes_accessed=1)


def halves(x):
    high = x.astype(BF16)
    return high, (x - high.astype(F32)).astype(BF16)


def dot(a, b, dims=((1,), (0,))):
    return lax.dot_general(a, b, (dims, ((), ())), preferred_element_type=F32)


def dot3(a, b, dims=((1,), (0,))):
    rows = a[0].shape[0]
    both = dot(jnp.concatenate(a, axis=0), b[0], dims)
    return both[:rows] + (dot(a[0], b[1], dims) + both[rows:])


def rows_of(pair, low, high):
    return pair[0][low:high], pair[1][low:high]


def unit_rows(x):
    return x * lax.rsqrt(jnp.sum(x * x, axis=-1, keepdims=True) + 1e-06)


def doc_ids(lengths_ref, first, shape, dim):
    place = first + lax.broadcasted_iota(jnp.int32, shape, dim)
    ids = jnp.zeros(shape, jnp.int32)
    before = jnp.int32(0)
    start = jnp.int32(0)
    for d in range(lengths_ref.shape[0]):
        ids = ids + (place >= start).astype(jnp.int32)
        before = before + (first > start).astype(jnp.int32)
        start = start + lengths_ref[d]
    return ids, before


def lanes_of(shape):
    return lax.broadcasted_iota(jnp.int32, shape, 1)


def side_by_side(system, count, size):
    lane = lanes_of((size, count)) // size
    side = system[:size]
    for b in range(1, count // size):
        side = jnp.where(lane == b, system[b * size : (b + 1) * size], side)
    return side


def tile_inverses(systems, count):
    sides = [side_by_side(s, count, TILE) for s in systems]
    whole = count // 128 * 128
    pieces = [s[:, low : low + 128] for s in sides for low in range(0, whole, 128)]
    rest = [s[:, whole:] for s in sides]
    if count > whole:
        for i in range(0, len(rest), 128 // (count - whole)):
            group = rest[i : i + 128 // (count - whole)]
            wide = sum(x.shape[1] for x in group)
            if wide < 128:
                group = group + [jnp.zeros((TILE, 128 - wide), F32)]
            pieces.append(jnp.concatenate(group, axis=1))
    lane = lanes_of((TILE, 128))
    home = lane - lane % TILE
    eye = (lane % TILE == lax.broadcasted_iota(jnp.int32, (TILE, 128), 0)).astype(F32)
    found = [[eye[8 * i : 8 * i + 8] for i in range(TILE // 8)] for _ in pieces]
    for j in range(TILE - 1):
        for p, piece in enumerate(pieces):
            line = found[p][j // 8][j % 8 : j % 8 + 1, :]
            for i in range((j + 1) // 8, TILE // 8):
                column = jnp.take_along_axis(
                    piece[8 * i : 8 * i + 8], home[:8] + j, axis=1, mode="promise_in_bounds"
                )
                found[p][i] = found[p][i] - column * line
    found = [jnp.concatenate(x, axis=0) for x in found]
    each = whole // 128
    results = []
    for h in range(len(systems)):
        parts = found[h * each : (h + 1) * each]
        if count > whole:
            per = 128 // (count - whole)
            at = h % per * (count - whole)
            parts = parts + [found[each * len(systems) + h // per][:, at : at + count - whole]]
        results.append(jnp.concatenate(parts, axis=1))
    return results


def spread(side, count, height, column_of):
    block = column_of(lanes_of(side.shape) // height)
    return jnp.concatenate([jnp.where(block == b, side, 0.0) for b in range(count // height)], axis=0)


def merged(system, side, count, size):
    lane = lanes_of(side.shape) // size
    even = lane % 2 == 0
    below = jnp.zeros(side.shape, F32)
    for b in range(1, count // size, 2):
        below = jnp.where(lane == b - 1, system[b * size : (b + 1) * size, :], below)
    wide = spread(side, count, size, lambda x: x)
    middle = dot3(halves(below), halves(wide))
    tall = spread(middle, count, size, lambda x: jnp.where(x % 2 == 0, x + 1, -1))
    corner = dot3(halves(jnp.where(even, 0.0, side)), halves(tall))
    return jnp.concatenate([jnp.where(even, side, 0.0), jnp.where(even, -corner, side)], axis=0)


def solve(systems, rights, count):
    sides = tile_inverses(systems, count)
    size = TILE
    while size < BLOCK:
        sides = [merged(s, x, count, size) for s, x in zip(systems, sides)]
        size = 2 * size
    wides = [halves(spread(x, count, BLOCK, lambda x: x)) for x in sides]
    row = lax.broadcasted_iota(jnp.int32, (count, count), 0) // BLOCK
    outside = row > lanes_of((count, count)) // BLOCK
    splits = [halves(jnp.where(outside, s, 0.0)) for s in systems]
    firsts = [dot3(w, r) for w, r in zip(wides, rights)]
    links = [halves(dot3(rows_of(w, BLOCK, count), s)) for w, s in zip(wides, splits)]
    done = [halves(x[:BLOCK]) for x in firsts]
    for b in range(1, count // BLOCK):
        low, high = b * BLOCK, (b + 1) * BLOCK
        for h in range(len(systems)):
            link = tuple(x[low - BLOCK : low, :low] for x in links[h])
            part = halves(firsts[h][low:high] - dot3(link, done[h]))
            done[h] = tuple(jnp.concatenate(x, axis=0) for x in zip(done[h], part))
    return done


def documents(lengths_ref, count, most, strict_ref, lower_ref, fresh_ref, flags_ref):
    first = lax.axis_index("ctx") * count
    ids_col, before = doc_ids(lengths_ref, first, (count, 1), 0)
    ids_row, _ = doc_ids(lengths_ref, first, (1, count), 1)
    row = lax.broadcasted_iota(jnp.int32, (count, count), 0)
    col = lanes_of((count, count))
    same = ids_col == ids_row
    lower_ref[...] = (same & (row >= col)).astype(F32)
    strict_ref[...] = (same & (row > col)).astype(F32)
    fresh_ref[...] = jnp.broadcast_to((ids_col == before).astype(F32), fresh_ref.shape)
    last = ids_row[:, count - 1 :]
    start = jnp.int32(0)
    latest = jnp.int32(0)
    for d in range(lengths_ref.shape[0]):
        latest = jnp.where(start < first, start, latest)
        start = start + lengths_ref[d]
    back = jnp.int32(0)
    for i in range(1, most):
        back = back + jnp.where(latest < first - i * count, 1, 0)
    flags_ref[0:1, :] = (ids_row == last).astype(F32)
    flags_ref[1:2, :] = jnp.broadcast_to((last == before).astype(F32), (1, count))
    flags_ref[2:3, :] = jnp.full((1, count), back.astype(F32))


def span_heads(head, k_ref, v_ref, beta_ref, g_ref, strict_ref, flags_ref, refs):
    count = k_ref.shape[0]
    up_ref, half_ref, kneg_refs, update_refs = refs[0], refs[1], refs[2:4], refs[4:6]
    width = refs[6].shape[1]
    places = [(a, b, i) for a, b in zip(refs[6::2], refs[7::2]) for i in range(a.shape[0])]
    heads = range(len(places))
    here = [slice((head + h) * width, (head + h + 1) * width) for h in heads]
    own = [slice(h * width, (h + 1) * width) for h in heads]
    row = lax.broadcasted_iota(jnp.int32, (count, count), 0)
    sums = (row >= lanes_of((count, count))).astype(F32).astype(BF16)
    cumul_all = dot(sums, g_ref[:, here[0].start : here[-1].stop])
    eye = lax.broadcasted_iota(jnp.int32, (width, width), 0) == lanes_of((width, width))
    strength = [beta_ref[head + h : head + h + 1, :] for h in heads]
    tail = flags_ref[0:1, :]
    kept = flags_ref[1:2, :width]
    total, kneg, kpos, khat, parts = [], [], [], [], []
    for h in heads:
        cumul = cumul_all[:, own[h]]
        total.append(cumul[count - 1 :, :])
        middle = total[h] * 0.5
        half = jnp.exp(middle)
        up = jnp.exp(cumul - middle)
        up_ref[:, own[h]] = up
        half_ref[0:1, own[h]] = half
        kn = unit_rows(k_ref[:, here[h]].astype(F32))
        negative = kn * jnp.exp(middle - cumul)
        kneg.append(halves(negative))
        for ref, x in zip(kneg_refs, kneg[h]):
            ref[:, own[h]] = x
        kpos.append(kn * up)
        parts.append(halves(kpos[h] * half))
        khat.append(halves((negative * half).T * (strength[h] * tail)))
    strict = strict_ref[...] > 0.0
    systems = [
        jnp.where(strict, dot3(halves(kpos[h]), kneg[h], ((1,), (1,))) * strength[h], 0.0)
        for h in heads
    ]
    rights = []
    for h in heads:
        value = v_ref[:, here[h]]
        rights.append(
            (
                jnp.concatenate([value, parts[h][0]], axis=1),
                jnp.concatenate([jnp.zeros_like(value), parts[h][1]], axis=1),
            )
        )
    updates = solve(systems, rights, count)
    for h in heads:
        for ref, x in zip(update_refs, updates[h]):
            ref[:, 2 * h * width : 2 * (h + 1) * width] = x
        found = dot3(khat[h], updates[h])
        a_ref, b_ref, i = places[h]
        b_ref[i] = found[:, :width]
        a_ref[i] = (jnp.where(eye, jnp.exp(total[h]), 0.0) - found[:, width:]) * kept


def query_kernel(head, q_ref, beta_ref, lower_ref, fresh_ref, flags_ref, *refs):
    up_ref, half_ref, kneg_refs, update_refs = refs[0], refs[1], refs[2:4], refs[4:6]
    out_ref, reach_ref = refs[6:]
    count, width = fresh_ref.shape
    heads = range(out_ref.shape[1] // width)
    own = [slice(h * width, (h + 1) * width) for h in heads]
    lower = lower_ref[...] > 0.0
    fresh = fresh_ref[...] > 0.0
    qpos = [
        unit_rows(q_ref[:, (head + h) * width : (head + h + 1) * width].astype(F32))
        * up_ref[:, own[h]]
        for h in heads
    ]
    scores = []
    for h in heads:
        kneg = tuple(x[:, own[h]] for x in kneg_refs)
        product = dot3(halves(qpos[h]), kneg, ((1,), (1,)))
        scores.append(
            halves(jnp.where(lower, product * beta_ref[head + h : head + h + 1, :], 0.0))
        )
    for h in heads:
        update = tuple(x[:, 2 * h * width : 2 * (h + 1) * width] for x in update_refs)
        found = dot3(scores[h], update)
        out_ref[:, own[h]] = found[:, :width]
        reach_ref[:, own[h]] = jnp.where(
            fresh, qpos[h] * half_ref[0:1, own[h]] - found[:, width:], 0.0
        )


def query(head, shared, flags, saved):
    beta, queries, _, _, _, _, lower, fresh = shared
    count = queries.shape[0]
    part = jax.ShapeDtypeStruct(saved[0].shape, F32)
    given = [queries, beta, lower, fresh, flags, *saved]
    return pl.pallas_call(
        functools.partial(query_kernel, head),
        in_specs=[VMEM] * len(given),
        out_specs=[VMEM] * 2,
        out_shape=[part, part],
        compiler_params=pltpu.CompilerParams(vmem_limit_bytes=32 << 20),
        cost_estimate=QUERY,
        name="query",
    )(*given)


VMEM = pl.BlockSpec(memory_space=pltpu.VMEM)
ANY = pl.BlockSpec(memory_space=pl.ANY)


def opening_kernel(most, *refs):
    lengths_hbm, beta_hbm, *sources = refs[:6]
    beta_ref, *targets = refs[6:11]
    masks = refs[11:15]
    outs = refs[15:-2]
    lengths_ref, sems = refs[-2:]
    count = sources[0].shape[0]
    cols = outs[0].shape[1]
    first = [(lengths_hbm, lengths_ref), (beta_hbm, beta_ref)]
    pairs = list(zip(sources, targets))
    first += [(x.at[:, :cols], y.at[:, :cols]) for x, y in pairs[1:]]
    rest = [(x.at[:, cols:], y.at[:, cols:]) for x, y in pairs[1:]] + pairs[:1]
    copies = [pltpu.make_async_copy(x, y, sems.at[i]) for i, (x, y) in enumerate(first + rest)]
    for copy in copies:
        copy.start()
    copies[0].wait()
    documents(lengths_ref, count, most, *masks)
    for copy in copies[1 : len(first)]:
        copy.wait()
    _, k_ref, v_ref, g_ref = targets
    strict_ref, _, _, flags_ref = masks
    span_heads(0, k_ref, v_ref, beta_ref, g_ref, strict_ref, flags_ref, outs)
    for copy in copies[len(first) :]:
        copy.wait()


def span_shapes(groups, count, width):
    cols = sum(groups) * width
    shapes = [((count, cols), F32), ((8, cols), F32)]
    shapes += [((count, cols), BF16)] * 2 + [((count, 2 * cols), BF16)] * 2
    shapes += [((x, width, width), F32) for x in groups for _ in range(2)]
    return [jax.ShapeDtypeStruct(*x) for x in shapes]


def opening(groups, most, lengths, strength, queries, keys, values, log_decay):
    count, total = queries.shape
    heads = strength.shape[0]
    width = total // heads
    given = [lengths, strength, queries, keys, values, log_decay]
    given = [pltpu.with_memory_space_constraint(x, pltpu.HBM) for x in given]
    square = jax.ShapeDtypeStruct((count, count), F32)
    kept = [jax.ShapeDtypeStruct(x.shape, x.dtype) for x in given[1:]]
    kept += [
        square,
        square,
        jax.ShapeDtypeStruct((count, width), F32),
        jax.ShapeDtypeStruct((8, count), F32),
    ]
    shapes = kept + span_shapes(groups, count, width)
    results = pl.pallas_call(
        functools.partial(opening_kernel, most),
        in_specs=[ANY] * len(given),
        out_specs=[VMEM] * len(shapes),
        out_shape=shapes,
        scratch_shapes=[pltpu.SMEM(lengths.shape, lengths.dtype), pltpu.SemaphoreType.DMA((9,))],
        compiler_params=pltpu.CompilerParams(vmem_limit_bytes=32 << 20),
        cost_estimate=COST,
        name="opening",
    )(*given)
    return results[: len(kept)], results[len(kept) :]


def span_kernel(head, k_ref, v_ref, beta_ref, g_ref, strict_ref, flags_ref, *refs):
    span_heads(head, k_ref, v_ref, beta_ref, g_ref, strict_ref, flags_ref, refs)


def span(head, groups, shared, flags):
    beta, queries, keys, values, decay, strict, _, _ = shared
    count = keys.shape[0]
    given = [keys, values, beta, decay, strict, flags]
    shapes = span_shapes(groups, count, keys.shape[1] // beta.shape[0])
    return pl.pallas_call(
        functools.partial(span_kernel, head),
        in_specs=[VMEM] * len(given),
        out_specs=[VMEM] * len(shapes),
        out_shape=shapes,
        compiler_params=pltpu.CompilerParams(vmem_limit_bytes=32 << 20),
        cost_estimate=COST,
        name="span",
    )(*given)


def pass_kernel(own, low, late, flags_ref, state_ref, *refs):
    out_ref = refs[-1]
    width = out_ref.shape[1]
    before = flags_ref[2:3, :width]
    kept = flags_ref[1:2, :width] > 0.0
    for h in range(out_ref.shape[0]):
        there = [i for i in range(late) if h < refs[own + 2 * i].shape[0]]
        sent = None
        if there:
            trans_a, trans_b = refs[own + 2 * there[0]][h], refs[own + 2 * there[0] + 1][h]
            for i in there[1:]:
                here = before == low + i
                trans_a = jnp.where(here, refs[own + 2 * i][h], trans_a)
                trans_b = jnp.where(here, refs[own + 2 * i + 1][h], trans_b)
            sent = trans_b + dot3(halves(trans_a), halves(state_ref[h]))
        if own and h < refs[0].shape[0]:
            sent = refs[0][h] if sent is None else jnp.where(kept, sent, refs[0][h])
        out_ref[h] = sent


def message(step, most, flags, trans_a, trans_b, received):
    own = [trans_b[step]] if step < len(trans_b) else []
    if step < LAG:
        return own[0]
    late = [step - LAG * i for i in range(1, most)]
    low = next(i for i, x in enumerate(late) if x < len(trans_b))
    late = [x for x in late if 0 <= x < len(trans_b)]
    carried = [x for g in late for x in (trans_a[g], trans_b[g])]
    size = max(x.shape[0] for x in own + carried)
    return pl.pallas_call(
        functools.partial(pass_kernel, len(own), low, len(late)),
        in_specs=[VMEM] * (2 + len(own) + len(carried)),
        out_specs=VMEM,
        out_shape=jax.ShapeDtypeStruct((size, *trans_b[0].shape[1:]), F32),
        compiler_params=pltpu.CompilerParams(vmem_limit_bytes=8 << 20),
        cost_estimate=PASS,
        name="pass_on",
    )(flags, received[step - LAG], *own, *carried)


def finish_kernel(parts, most, flags_ref, gain_ref, *refs):
    mixed_hbm, buffer, sems = refs[-3:]
    width = refs[2].shape[1]
    before = flags_ref[2:3, :width]
    copies, filled = [], 0
    for n, (head, at, size) in enumerate(parts):
        outs_ref, reach_ref, *states = refs[n * (most + 2) : (n + 1) * (most + 2)]
        for h in range(size):
            here = slice((at + h) * width, (at + h + 1) * width)
            state = states[0][h]
            for i in range(1, most):
                state = jnp.where(before == i, states[i][h], state)
            total = outs_ref[:, here] + dot3(halves(reach_ref[:, here]), halves(state))
            scale = lax.rsqrt(jnp.mean(total * total, axis=-1, keepdims=True) + 1e-06)
            there = slice((head + h) * width, (head + h + 1) * width)
            place = slice((filled + h) * width, (filled + h + 1) * width)
            buffer[:, place] = (total * scale * gain_ref[:, there]).astype(BF16)
        there = slice(head * width, (head + size) * width)
        place = slice(filled * width, (filled + size) * width)
        copies.append(
            pltpu.make_async_copy(buffer.at[:, place], mixed_hbm.at[:, there], sems.at[n])
        )
        copies[-1].start()
        filled += size
    for copy in copies:
        copy.wait()


def finished(chosen, places, mixed, flags, answers, received, most, gain):
    count = answers[0][0].shape[0]
    width = received[0].shape[1]
    given = [flags, gain]
    for g in chosen:
        given += [*answers[g], *(received[g + LAG * i] for i in range(most))]
    specs = [VMEM] * len(given)
    aliases = {}
    parts = [places[g] for g in chosen]
    kernel = functools.partial(finish_kernel, parts, most)
    if mixed is not None:
        aliases = {len(given): 0}
        given.append(mixed)
        specs.append(ANY)
        kernel = functools.partial(finish_more, parts, most)
    return pl.pallas_call(
        kernel,
        in_specs=specs,
        out_specs=pl.BlockSpec(memory_space=pltpu.HBM),
        out_shape=jax.ShapeDtypeStruct((count, gain.shape[1]), BF16),
        scratch_shapes=[
            pltpu.VMEM((count, sum(x[2] for x in parts) * width), BF16),
            pltpu.SemaphoreType.DMA((len(parts),)),
        ],
        input_output_aliases=aliases,
        compiler_params=pltpu.CompilerParams(vmem_limit_bytes=16 << 20),
        cost_estimate=END,
        name="finish",
    )(*given)


def finish_more(parts, most, *refs):
    finish_kernel(parts, most, *refs[:-4], *refs[-3:])


def then(flags, results):
    flags, results = lax.optimization_barrier((flags, tuple(results)))
    return flags, list(results)


def local(queries, keys, values, beta, log_decay, out_gain, doc_lengths):
    devices = lax.axis_size("ctx")
    ring = [(i, (i + 1) % devices) for i in range(devices)]
    most = devices // 2
    gain = out_gain.reshape(1, -1)
    sizes = [x for s in SPANS for x in s]
    groups = len(sizes)
    places, spans, head = [], [], 0
    for n, span_groups in enumerate(SPANS):
        for i, size in enumerate(span_groups):
            places.append((head + sum(span_groups[:i]), sum(span_groups[:i]), size))
            spans.append(n)
        head += sum(span_groups)
    shared, first = opening(SPANS[0], most, doc_lengths, beta.T, queries, keys, values, log_decay)
    shared, flags = shared[:-1], shared[-1]
    flags, first = then(flags, first)
    found = [first]
    trans_a, trans_b = first[6::2], first[7::2]
    received = []
    mixed = None
    answers = []
    starts = [sum(map(sum, SPANS[:n])) for n in range(len(SPANS))]
    for step in range(groups + LAG * (most - 1)):
        if step < groups and spans[step] == len(found):
            flags, results = then(flags, span(places[step][0], SPANS[spans[step]], shared, flags))
            found.append(results)
            trans_a, trans_b = trans_a + results[6::2], trans_b + results[7::2]
        sent = message(step, most, flags, trans_a, trans_b, received)
        if step >= LAG:
            flags, (sent,) = then(flags, [sent])
        received.append(lax.ppermute(sent, "ctx", ring))
        for _ in range(FILL[max(0, step - groups + 1)] if step >= groups - 1 else 0):
            if len(answers) < len(found):
                n = len(answers)
                flags, results = then(flags, query(starts[n], shared, flags, found[n][:6]))
                answers.append(results)
    for n in range(len(answers), len(found)):
        flags, results = then(flags, query(starts[n], shared, flags, found[n][:6]))
        answers.append(results)
    answers = [answers[n] for n in spans]
    for chosen in (range(groups - LATE), *([g] for g in range(groups - LATE, groups))):
        mixed = finished(chosen, places, mixed, flags, answers, received, most, gain)
    return mixed


def solution(mesh):
    rows = P(("dp", "ctx"), None)
    return jax.shard_map(
        local,
        mesh=mesh,
        in_specs=(rows, rows, rows, rows, rows, P(), P("dp")),
        out_specs=rows,
        check_vma=False,
    )
```
